256 devices in a mesh: dp: 32 (over y, x, core), mp: 8 (over z).
Axes of the slice: x: 4, y: 4, z: 8, core: 2. Of those that a mesh axis runs over, the one named last changes fastest.
Arguments:
- acts: bfloat16 [8192, 8192], P('dp', 'mp'), may hold values from -6 to 6
- grads: bfloat16 [8192, 28672], P('dp', 'mp'), may hold values from -6 to 6
- proj_in: bfloat16 [8192, 64], replicated, may hold values from -0.0625 to 0.0625
- block_vals: bfloat16 [128, 128, 64], replicated, may hold values from -0.046875 to 0.046875
- block_index: int32 [128], replicated, may hold values from 0 to 223, as said below
- assign: int32 [32, 256], P('dp'), may hold values from 0 to 255, each once within a row
Outputs:
- features: bfloat16 [8192, 4096], P(('dp', 'mp'))
- factor: float32 [8, 512, 512], P('mp')
The draws below stay inside these ranges and needn't reach their ends.
Inputs may be any that keep to these rules, and one draw needn't show every extreme that they name: `block_index`: 128 distinct row blocks. Each row of assign names every example of its group once.
All inputs are finite; a program needn't handle non-finite values.
Results may differ from the reference program's by a relative error of at most 0.013.
Values may be sent and summed in bfloat16 or wider, within the bound.
No kernel may reach another device: no remote copies, remote signals or barrier semaphores. Data moves between devices by JAX's collectives and lax.ppermute only.
A program may use at most 64 MiB of HBM per device.

```python
import jax
import jax.numpy as jnp
from jax import lax

D = 8192
FF = 28672
K_IN = 64
K_OUT = 64
BLK = 128
NBLK = 128
FB = 512
FEAT = 4096
NBLOCKS = 224
E_DP = 256
GROUPS = 32
EXAMPLES = 8192


def draw_block_index(key, part):
    return jax.random.permutation(key, FF // BLK)[:NBLK].astype(jnp.int32)


def levels(stream_key, shape, split, least, high):
    factor_of, own = 1.0, jax.random.fold_in(stream_key, 6)
    for axis_at, blocks in split:
        steps = jnp.exp(jax.random.uniform(jax.random.fold_in(own, axis_at), (blocks,), jnp.float32, least / len(split), high / len(split)))
        factor_of = factor_of * jnp.repeat(steps, shape[axis_at] // blocks).reshape([-1 if axis == axis_at else 1 for axis in range(len(shape))])
    return factor_of


def scatter_about(key, dims, scale, most, split=(), kind=jnp.bfloat16):
    entries = scale * jax.random.normal(key, dims, jnp.float32)
    if split:
        entries = entries * levels(key, dims, split, -0.22, 0.18)
    return jnp.clip(entries, -most, most).astype(kind)


def setup_inputs(seed: int = 0) -> dict:
    splits = jax.random.split(jax.random.key(seed), 7)
    return {
        "acts": scatter_about(splits[0], (EXAMPLES, D), 1.0, 6.0, ((0, 32), (1, 8))),
        "grads": scatter_about(splits[1], (EXAMPLES, FF), 1.0, 6.0, ((0, 32), (1, 8))),
        "proj_in": scatter_about(splits[2], (D, K_IN), D ** -0.5, 0.0625),
        "block_vals": scatter_about(splits[3], (NBLK, BLK, K_OUT), (NBLK * BLK) ** -0.5, 0.046875),
        "block_index": draw_block_index(jax.random.fold_in(splits[6], 71), 0),
        "assign": jax.vmap(lambda own: jax.random.permutation(own, E_DP))(jax.random.split(splits[5], GROUPS)).reshape((GROUPS, E_DP)).astype(jnp.int32),
    }


def reference(acts, grads, proj_in, block_vals, block_index, assign):

    def one_group(group):
        rows = assign[group].astype(jnp.int32) + (group * E_DP).astype(jnp.int32)
        ordered_acts = jnp.take(acts, rows, axis=0)
        ordered_grads = jnp.take(grads, rows, axis=0)
        in_coords = jnp.dot(ordered_acts.astype(jnp.float32), proj_in.astype(jnp.float32), preferred_element_type=jnp.float32).astype(jnp.bfloat16)
        grid = ordered_grads.reshape(E_DP, NBLOCKS, BLK)
        picked = jnp.take(grid, block_index, axis=1)
        out_coords = jnp.einsum('rtk,tko->ro', picked.astype(jnp.float32), block_vals.astype(jnp.float32)).astype(jnp.bfloat16)
        outer = in_coords.astype(jnp.float32)[:, :, None] * out_coords.astype(jnp.float32)[:, None, :]
        return outer.reshape(E_DP, FEAT).astype(jnp.bfloat16)
    features = lax.map(one_group, jnp.arange(GROUPS, dtype=jnp.int32)).reshape(EXAMPLES, FEAT)

    def one_block(block):
        columns = lax.dynamic_slice_in_dim(features, (block * FB).astype(jnp.int32), FB, 1)
        return jnp.dot(columns.T.astype(jnp.float32), columns.astype(jnp.float32), preferred_element_type=jnp.float32)
    gram = lax.map(one_block, jnp.arange(FEAT // FB, dtype=jnp.int32))
    identity = jnp.eye(FB, dtype=jnp.float32)
    covariance = gram / EXAMPLES + 0.05 * identity
    lower = jnp.linalg.cholesky(covariance)
    factor = jnp.swapaxes(lower, 1, 2)
    return (features, factor)
```

```python
import functools

import jax
import jax.numpy as jnp
from jax import lax
from jax.experimental import pallas as pl
from jax.experimental.pallas import tpu as pltpu
from jax.sharding import PartitionSpec as P

FB = 512
DAMPING = 0.05
BF16 = jnp.bfloat16
F32 = jnp.float32
NT = (((1,), (1,)), ((), ()))


def nt_dot(a, b):
    return lax.dot_general(a, b, NT, preferred_element_type=F32)


def project_kernel(index_ref, assign_ref, acts_hbm, grads_hbm, proj_hbm, vals_hbm, send_ref,
                   acts, grads, proj, vals, flags, sems, val_sems):
    me = lax.axis_index("mp")
    k_in = acts.shape[1]
    blocks = val_sems.shape[0]
    copies = (
        pltpu.make_async_copy(proj_hbm.at[:, pl.ds(pl.multiple_of(me * k_in, 128), k_in)], proj, sems.at[0]),
        pltpu.make_async_copy(acts_hbm, acts, sems.at[1]),
        pltpu.make_async_copy(grads_hbm, grads, sems.at[2]),
    )
    for copy in copies:
        copy.start()

    def clear(j, carry):
        flags[j] = -1
        return carry

    lax.fori_loop(0, blocks, clear, 0)

    def value_copy(j, t):
        return pltpu.make_async_copy(
            vals_hbm.at[t], vals.at[:, pl.ds(pl.multiple_of(j * 128, 128), 128)], val_sems.at[j])

    def find(t, carry):
        j = index_ref[t] - me * blocks

        @pl.when((j >= 0) & (j < blocks))
        def _():
            flags[j] = t
            value_copy(j, t).start()

        return carry

    lax.fori_loop(0, index_ref.shape[0], find, 0)

    def blank(j, carry):
        @pl.when(flags[j] < 0)
        def _():
            vals[:, pl.ds(pl.multiple_of(j * 128, 128), 128)] = jnp.zeros((vals.shape[0], 128), BF16)

        return carry

    lax.fori_loop(0, blocks, blank, 0)

    examples = acts.shape[0]
    rows = lax.broadcasted_iota(jnp.int32, (examples, examples), 0)
    order = jnp.where(rows == assign_ref[...], 1.0, 0.0).astype(BF16)
    copies[0].wait()
    copies[1].wait()
    in_part = nt_dot(proj[...], acts[...]).astype(BF16)
    in_part = jnp.dot(in_part, order, preferred_element_type=F32)

    def settle(j, carry):
        @pl.when(flags[j] >= 0)
        def _():
            value_copy(j, flags[j]).wait()

        return carry

    lax.fori_loop(0, blocks, settle, 0)
    copies[2].wait()
    out_part = nt_dot(vals[...], grads[...]).astype(BF16)
    out_part = jnp.dot(out_part, order, preferred_element_type=F32)
    for c in range(send_ref.shape[0]):
        send_ref[c, 0:64, :] = out_part[:, 0:128].astype(BF16)
        send_ref[c, 64:128, :] = out_part[:, 128:256].astype(BF16)
        tops = jnp.concatenate([in_part[8 * c:8 * c + 8, 0:128], in_part[8 * c:8 * c + 8, 128:256]], axis=0)
        send_ref[c, 128:144, :] = tops.astype(BF16)
        mine = jnp.concatenate(
            [in_part[16 * k:16 * k + 16, 32 * c:32 * c + 32] for k in range(4)], axis=1)
        send_ref[c, 144:160, :] = mine.astype(BF16)


TILES = [(i, j) for i in range(4) for j in range(i, 4)]


def gram_kernel(recv_ref, coords_ref, keep_ref, give_ref, ft, packed):
    total = recv_ref[0].astype(F32)
    for c in range(1, recv_ref.shape[0]):
        total = total + recv_ref[c].astype(F32)
    coords = total.astype(BF16)
    coords_ref[...] = coords
    wide = coords.astype(F32)
    out_t = (wide[0:64], wide[64:128])
    in_t = (wide[128:136], wide[136:144])
    for p in range(8):
        for h in range(2):
            ft[64 * p:64 * p + 64, 128 * h:128 * h + 128] = (in_t[h][p:p + 1] * out_t[h]).astype(BF16)
    for at, (i, j) in enumerate(TILES):
        packed[128 * at:128 * at + 128, :] = nt_dot(
            ft[128 * i:128 * i + 128, :], ft[128 * j:128 * j + 128, :]).astype(BF16)
    core = lax.rem(lax.axis_index("dp"), 2)
    half = packed.shape[0] // 2
    keep_ref[...] = packed[pl.ds(pl.multiple_of(core * half, half), half), :]
    give_ref[...] = packed[pl.ds(pl.multiple_of((1 - core) * half, half), half), :]


def features_kernel(coords_ref, features_ref):
    me = lax.axis_index("mp")
    coords = coords_ref[...]
    picked = jnp.concatenate([coords[0:64], coords[64:128]], axis=1)
    rows = lax.broadcasted_iota(jnp.int32, (32, 256), 0)
    cols = lax.broadcasted_iota(jnp.int32, (32, 256), 1)
    pick = jnp.where(cols == rows + 32 * me, 1.0, 0.0).astype(BF16)
    outs = nt_dot(pick, picked)
    wide = coords[144:160].astype(F32)
    mine = jnp.concatenate([wide[:, 32 * k:32 * k + 32] for k in range(4)], axis=0).astype(BF16)
    turn = jnp.where(
        lax.broadcasted_iota(jnp.int32, (32, 32), 0) == lax.broadcasted_iota(jnp.int32, (32, 32), 1),
        1.0, 0.0).astype(BF16)
    ins = nt_dot(turn, mine).astype(BF16)
    both = jnp.concatenate([outs, outs], axis=1)
    step = 512
    for at in range(features_ref.shape[1] // step):
        p = lax.broadcasted_iota(jnp.int32, (64, step), 0)
        f = lax.broadcasted_iota(jnp.int32, (64, step), 1)
        spread = jnp.where(p == (step // 64) * at + lax.div(f, 64), 1.0, 0.0).astype(BF16)
        left = jnp.dot(ins, spread, preferred_element_type=F32)
        for w in range(step // 128):
            features_ref[:, step * at + 128 * w:step * at + 128 * w + 128] = (
                left[:, 128 * w:128 * w + 128] * both).astype(BF16)


def spot(y, x, core):
    return (y * 4 + x) * 2 + core


def moves(step):
    return [(spot(y, x, c), spot(*step(y, x, c)))
            for y in range(4) for x in range(4) for c in range(2)]


def shards(acts, grads, proj_in, block_vals, block_index, assign):
    ex, k_in = acts.shape
    k_out = grads.shape[1]
    any_spec = pl.BlockSpec(memory_space=pl.ANY)
    vmem = pl.BlockSpec(memory_space=pltpu.VMEM)
    smem = pl.BlockSpec(memory_space=pltpu.SMEM)
    send = pl.pallas_call(
        project_kernel,
        out_shape=jax.ShapeDtypeStruct((8, 160, 128), BF16),
        in_specs=[smem, vmem, any_spec, any_spec, any_spec, any_spec],
        out_specs=vmem,
        scratch_shapes=[
            pltpu.VMEM((ex, k_in), BF16),
            pltpu.VMEM((ex, k_out), BF16),
            pltpu.VMEM((64, k_in), BF16),
            pltpu.VMEM((64, k_out), BF16),
            pltpu.SMEM((k_out // 128,), jnp.int32),
            pltpu.SemaphoreType.DMA((3,)),
            pltpu.SemaphoreType.DMA((k_out // 128,)),
        ],
        name="project",
    )(block_index, assign, acts, grads, proj_in.T, jnp.swapaxes(block_vals, 1, 2))
    recv = lax.all_to_all(send, "mp", 0, 0, tiled=True)
    coords, keep, give = pl.pallas_call(
        gram_kernel,
        out_shape=(
            jax.ShapeDtypeStruct((160, 128), BF16),
            jax.ShapeDtypeStruct((640, 128), BF16),
            jax.ShapeDtypeStruct((640, 128), BF16),
        ),
        in_specs=[vmem],
        out_specs=(vmem, vmem, vmem),
        scratch_shapes=[pltpu.VMEM((FB, 256), BF16), pltpu.VMEM((1280, 128), BF16)],
        name="gram",
    )(recv)
    features = pl.pallas_call(
        features_kernel,
        out_shape=jax.ShapeDtypeStruct((32, 4096), BF16),
        in_specs=[vmem],
        out_specs=vmem,
        cost_estimate=pl.CostEstimate(flops=2 * 32 * 64 * 4096, bytes_accessed=300000, transcendentals=0),
        name="features",
    )(coords)
    total = keep + lax.ppermute(give, "dp", moves(lambda y, x, c: (y, x, 1 - c)))
    for step in (
        lambda y, x, c: (y, x ^ 1, c),
        lambda y, x, c: (y, 3 - x, c),
        lambda y, x, c: (y ^ 1, x, c),
        lambda y, x, c: (3 - y, x, c),
    ):
        total = total + lax.ppermute(total, "dp", moves(step))
    other = lax.ppermute(total, "dp", moves(lambda y, x, c: (y, x, 1 - c)))
    core = lax.rem(lax.axis_index("dp"), 2)
    packed = jnp.where(core == 0, jnp.concatenate([total, other]), jnp.concatenate([other, total]))
    tiles = packed.reshape(10, 128, 128).astype(F32)
    grid = {}
    for at, (i, j) in enumerate(TILES):
        grid[i, j] = tiles[at]
        if i != j:
            grid[j, i] = tiles[at].T
    gram = jnp.concatenate([jnp.concatenate([grid[i, j] for j in range(4)], axis=1) for i in range(4)])
    cov = gram / 8192 + DAMPING * jnp.eye(FB, dtype=F32)
    factor = jnp.swapaxes(jnp.linalg.cholesky(cov[None]), 1, 2)
    return features, factor


def solution(mesh):
    return jax.shard_map(
        shards,
        mesh=mesh,
        in_specs=(P("dp", "mp"), P("dp", "mp"), P(), P(), P(), P("dp", None)),
        out_specs=(P(("dp", "mp"), None), P("mp", None, None)),
        check_vma=False,
    )
```

```python
import functools

import jax
import jax.numpy as jnp
from jax import lax
from jax.experimental import pallas as pl
from jax.experimental.pallas import tpu as pltpu
from jax.sharding import PartitionSpec as P

FB = 512
DAMPING = 0.05
BF16 = jnp.bfloat16
F32 = jnp.float32
NT = (((1,), (1,)), ((), ()))


def nt_dot(a, b):
    return lax.dot_general(a, b, NT, preferred_element_type=F32)


def project_kernel(index_ref, assign_ref, acts_hbm, grads_hbm, proj_hbm, vals_hbm, send_ref,
                   acts, grads, proj, vals, flags, sems, val_sems):
    me = lax.axis_index("mp")
    k_in = acts.shape[1]
    blocks = val_sems.shape[0]
    copies = (
        pltpu.make_async_copy(proj_hbm.at[:, pl.ds(pl.multiple_of(me * k_in, 128), k_in)], proj, sems.at[0]),
        pltpu.make_async_copy(acts_hbm, acts, sems.at[1]),
        pltpu.make_async_copy(grads_hbm, grads, sems.at[2]),
    )
    for copy in copies:
        copy.start()

    def clear(j, carry):
        flags[j] = -1
        return carry

    lax.fori_loop(0, blocks, clear, 0)

    def value_copy(j, t):
        return pltpu.make_async_copy(
            vals_hbm.at[t], vals.at[:, pl.ds(pl.multiple_of(j * 128, 128), 128)], val_sems.at[j])

    def find(t, carry):
        j = index_ref[t] - me * blocks

        @pl.when((j >= 0) & (j < blocks))
        def _():
            flags[j] = t
            value_copy(j, t).start()

        return carry

    lax.fori_loop(0, index_ref.shape[0], find, 0)

    def blank(j, carry):
        @pl.when(flags[j] < 0)
        def _():
            vals[:, pl.ds(pl.multiple_of(j * 128, 128), 128)] = jnp.zeros((vals.shape[0], 128), BF16)

        return carry

    lax.fori_loop(0, blocks, blank, 0)

    examples = acts.shape[0]
    rows = lax.broadcasted_iota(jnp.int32, (examples, examples), 0)
    order = jnp.where(rows == assign_ref[...], 1.0, 0.0).astype(BF16)
    copies[0].wait()
    copies[1].wait()
    in_part = nt_dot(proj[...], acts[...]).astype(BF16)
    in_part = jnp.dot(in_part, order, preferred_element_type=F32)

    def settle(j, carry):
        @pl.when(flags[j] >= 0)
        def _():
            value_copy(j, flags[j]).wait()

        return carry

    lax.fori_loop(0, blocks, settle, 0)
    copies[2].wait()
    out_part = nt_dot(vals[...], grads[...]).astype(BF16)
    out_part = jnp.dot(out_part, order, preferred_element_type=F32)
    for c in range(send_ref.shape[0]):
        send_ref[c, 0:64, :] = out_part[:, 0:128].astype(BF16)
        send_ref[c, 64:128, :] = out_part[:, 128:256].astype(BF16)
        tops = jnp.concatenate([in_part[8 * c:8 * c + 8, 0:128], in_part[8 * c:8 * c + 8, 128:256]], axis=0)
        send_ref[c, 128:144, :] = tops.astype(BF16)
        mine = jnp.concatenate(
            [in_part[16 * k:16 * k + 16, 32 * c:32 * c + 32] for k in range(4)], axis=1)
        send_ref[c, 144:160, :] = mine.astype(BF16)


TILES = [(i, j) for i in range(4) for j in range(i, 4)]


def gram_kernel(recv_ref, coords_ref, keep_ref, give_ref, ft, packed):
    total = recv_ref[0].astype(F32)
    for c in range(1, recv_ref.shape[0]):
        total = total + recv_ref[c].astype(F32)
    coords = total.astype(BF16)
    coords_ref[...] = coords
    wide = coords.astype(F32)
    out_t = (wide[0:64], wide[64:128])
    in_t = (wide[128:136], wide[136:144])
    for p in range(8):
        for h in range(2):
            ft[64 * p:64 * p + 64, 128 * h:128 * h + 128] = (in_t[h][p:p + 1] * out_t[h]).astype(BF16)
    for at, (i, j) in enumerate(TILES):
        packed[128 * at:128 * at + 128, :] = nt_dot(
            ft[128 * i:128 * i + 128, :], ft[128 * j:128 * j + 128, :]).astype(BF16)
    core = lax.rem(lax.axis_index("dp"), 2)
    half = packed.shape[0] // 2
    keep_ref[...] = packed[pl.ds(pl.multiple_of(core * half, half), half), :]
    give_ref[...] = packed[pl.ds(pl.multiple_of((1 - core) * half, half), half), :]


def features_kernel(coords_ref, features_ref):
    me = lax.axis_index("mp")
    coords = coords_ref[...]
    picked = jnp.concatenate([coords[0:64], coords[64:128]], axis=1)
    rows = lax.broadcasted_iota(jnp.int32, (32, 256), 0)
    cols = lax.broadcasted_iota(jnp.int32, (32, 256), 1)
    pick = jnp.where(cols == rows + 32 * me, 1.0, 0.0).astype(BF16)
    outs = nt_dot(pick, picked)
    wide = coords[144:160].astype(F32)
    mine = jnp.concatenate([wide[:, 32 * k:32 * k + 32] for k in range(4)], axis=0).astype(BF16)
    turn = jnp.where(
        lax.broadcasted_iota(jnp.int32, (32, 32), 0) == lax.broadcasted_iota(jnp.int32, (32, 32), 1),
        1.0, 0.0).astype(BF16)
    ins = nt_dot(turn, mine).astype(BF16)
    both = jnp.concatenate([outs, outs], axis=1)
    step = 512
    for at in range(features_ref.shape[1] // step):
        p = lax.broadcasted_iota(jnp.int32, (64, step), 0)
        f = lax.broadcasted_iota(jnp.int32, (64, step), 1)
        spread = jnp.where(p == (step // 64) * at + lax.div(f, 64), 1.0, 0.0).astype(BF16)
        left = jnp.dot(ins, spread, preferred_element_type=F32)
        for w in range(step // 128):
            features_ref[:, step * at + 128 * w:step * at + 128 * w + 128] = (
                left[:, 128 * w:128 * w + 128] * both).astype(BF16)


def spread_lane(x, at):
    return jnp.take_along_axis(x, jnp.full((8, 128), at, jnp.int32), axis=1)

def row(x, j):
    return jnp.broadcast_to(x[j:j + 1, :], (8, 128))

def factor_block(c):
    sub = lax.broadcasted_iota(jnp.int32, (8, 128), 0)
    lane = lax.broadcasted_iota(jnp.int32, (8, 128), 1)
    n = len(c)
    upper, inverse = [], []
    for p in range(n):
        base = 8 * p
        inside = (lane >= base) & (lane < base + 8)
        cols = [spread_lane(c[p], base + k) for k in range(8)]
        own = c[p]
        aug = jnp.where(inside, jnp.where(lane - base == sub, 1.0, 0.0), c[p])
        zed = aug
        below = {t: [spread_lane(c[t], base + k) for k in range(8)] for t in range(p + 1, n)}
        inv = jnp.zeros((8, 128), F32)
        for j in range(8):
            r = 1.0 / row(cols[j], j)
            inv = jnp.where(sub == j, r, inv)
            full = jnp.where(sub == j, 0.0, cols[j])
            part = jnp.where(sub > j, cols[j], 0.0)
            for k in range(j + 1, 8):
                cols[k] = cols[k] - (full * row(cols[k], j)) * r
            ro, ra, rz = row(own, j), row(aug, j), row(zed, j)
            own = own - (part * ro) * r
            aug = aug - (part * ra) * r
            zed = zed - (full * rz) * r
        zed = zed * inv
        root = jnp.sqrt(inv)
        upper.append(jnp.where(lane >= base + sub, own * root, 0.0))
        inverse.append(jnp.where(lane <= base + sub, aug * root, 0.0))
        rows = [row(zed, k) for k in range(8)]
        for t in range(p + 1, n):
            s = [below[t][k] * rows[k] for k in range(8)]
            s = ((s[0] + s[1]) + (s[2] + s[3])) + ((s[4] + s[5]) + (s[6] + s[7]))
            c[t] = jnp.where(inside, 0.0, c[t]) - s
    return upper, inverse

def factor_kernel(total_ref, other_ref, out_ref, work, inv):
    core = lax.rem(lax.axis_index("dp"), 2)
    half = total_ref.shape[0]
    at0 = pl.multiple_of(core * half, half); at1 = pl.multiple_of((1 - core) * half, half)
    work[pl.ds(at0, half), :] = total_ref[...].astype(F32) * (1.0 / 8192)
    work[pl.ds(at1, half), :] = other_ref[...].astype(F32) * (1.0 / 8192)
    place = {ij: 128 * n for n, ij in enumerate(TILES)}
    sub = lax.broadcasted_iota(jnp.int32, (8, 128), 0)
    lane = lax.broadcasted_iota(jnp.int32, (8, 128), 1)
    for s in range(4):
        o = place[s, s]
        c = [work[o + 8 * t:o + 8 * t + 8, :] + jnp.where(lane == sub + 8 * t, DAMPING, 0.0) for t in range(16)]
        upper, inverse = factor_block(c)
        for t in range(16):
            out_ref[128 * s + 8 * t:128 * s + 8 * t + 8, 128 * s:128 * s + 128] = upper[t]
            inv[8 * t:8 * t + 8, :] = inverse[t]
        for j in range(s):
            out_ref[128 * s:128 * s + 128, 128 * j:128 * j + 128] = jnp.zeros((128, 128), F32)
        for j in range(s + 1, 4):
            a = work[place[s, j]:place[s, j] + 128, :]
            out_ref[128 * s:128 * s + 128, 128 * j:128 * j + 128] = jnp.dot(
                inv[...], a, preferred_element_type=F32, precision=lax.Precision.HIGHEST)
        for i in range(s + 1, 4):
            for j in range(i, 4):
                ri = out_ref[128 * s:128 * s + 128, 128 * i:128 * i + 128]
                rj = out_ref[128 * s:128 * s + 128, 128 * j:128 * j + 128]
                work[place[i, j]:place[i, j] + 128, :] -= lax.dot_general(
                    ri, rj, (((0,), (0,)), ((), ())), preferred_element_type=F32, precision=lax.Precision.HIGHEST)

def spot(y, x, core):
    return (y * 4 + x) * 2 + core


def moves(step):
    return [(spot(y, x, c), spot(*step(y, x, c)))
            for y in range(4) for x in range(4) for c in range(2)]


def shards(acts, grads, proj_in, block_vals, block_index, assign):
    ex, k_in = acts.shape
    k_out = grads.shape[1]
    any_spec = pl.BlockSpec(memory_space=pl.ANY)
    vmem = pl.BlockSpec(memory_space=pltpu.VMEM)
    smem = pl.BlockSpec(memory_space=pltpu.SMEM)
    send = pl.pallas_call(
        project_kernel,
        out_shape=jax.ShapeDtypeStruct((8, 160, 128), BF16),
        in_specs=[smem, vmem, any_spec, any_spec, any_spec, any_spec],
        out_specs=vmem,
        scratch_shapes=[
            pltpu.VMEM((ex, k_in), BF16),
            pltpu.VMEM((ex, k_out), BF16),
            pltpu.VMEM((64, k_in), BF16),
            pltpu.VMEM((64, k_out), BF16),
            pltpu.SMEM((k_out // 128,), jnp.int32),
            pltpu.SemaphoreType.DMA((3,)),
            pltpu.SemaphoreType.DMA((k_out // 128,)),
        ],
        name="project",
    )(block_index, assign, acts, grads, proj_in.T, jnp.swapaxes(block_vals, 1, 2))
    recv = lax.all_to_all(send, "mp", 0, 0, tiled=True)
    coords, keep, give = pl.pallas_call(
        gram_kernel,
        out_shape=(
            jax.ShapeDtypeStruct((160, 128), BF16),
            jax.ShapeDtypeStruct((640, 128), BF16),
            jax.ShapeDtypeStruct((640, 128), BF16),
        ),
        in_specs=[vmem],
        out_specs=(vmem, vmem, vmem),
        scratch_shapes=[pltpu.VMEM((FB, 256), BF16), pltpu.VMEM((1280, 128), BF16)],
        name="gram",
    )(recv)
    features = pl.pallas_call(
        features_kernel,
        out_shape=jax.ShapeDtypeStruct((32, 4096), BF16),
        in_specs=[vmem],
        out_specs=vmem,
        cost_estimate=pl.CostEstimate(flops=2 * 32 * 64 * 4096, bytes_accessed=300000, transcendentals=0),
        name="features",
    )(coords)
    total = keep + lax.ppermute(give, "dp", moves(lambda y, x, c: (y, x, 1 - c)))
    for step in (
        lambda y, x, c: (y, x ^ 1, c),
        lambda y, x, c: (y, 3 - x, c),
        lambda y, x, c: (y ^ 1, x, c),
        lambda y, x, c: (3 - y, x, c),
    ):
        total = total + lax.ppermute(total, "dp", moves(step))
        total, features = lax.optimization_barrier((total, features))
    other = lax.ppermute(total, "dp", moves(lambda y, x, c: (y, x, 1 - c)))
    factor = pl.pallas_call(
        factor_kernel,
        out_shape=jax.ShapeDtypeStruct((FB, FB), F32),
        in_specs=[vmem, vmem],
        out_specs=vmem,
        scratch_shapes=[pltpu.VMEM((1280, 128), F32), pltpu.VMEM((128, 128), F32)],
        name="factor",
    )(total, other).reshape(1, FB, FB)
    return features, factor


def solution(mesh):
    return jax.shard_map(
        shards,
        mesh=mesh,
        in_specs=(P("dp", "mp"), P("dp", "mp"), P(), P(), P(), P("dp", None)),
        out_specs=(P(("dp", "mp"), None), P("mp", None, None)),
        check_vma=False,
    )
```

```python
import functools

import jax
import jax.numpy as jnp
from jax import lax
from jax.experimental import pallas as pl
from jax.experimental.pallas import tpu as pltpu
from jax.sharding import PartitionSpec as P

FB = 512
DAMPING = 0.05
BF16 = jnp.bfloat16
F32 = jnp.float32
NT = (((1,), (1,)), ((), ()))


def nt_dot(a, b):
    return lax.dot_general(a, b, NT, preferred_element_type=F32)


def project_kernel(index_ref, assign_ref, acts_hbm, grads_hbm, proj_hbm, vals_hbm, send_ref,
                   acts, grads, proj, vals, flags, sems, val_sems):
    me = lax.axis_index("mp")
    k_in = acts.shape[1]
    blocks = val_sems.shape[0]
    copies = (
        pltpu.make_async_copy(proj_hbm.at[:, pl.ds(pl.multiple_of(me * k_in, 128), k_in)], proj, sems.at[0]),
        pltpu.make_async_copy(acts_hbm, acts, sems.at[1]),
        pltpu.make_async_copy(grads_hbm, grads, sems.at[2]),
    )
    for copy in copies:
        copy.start()

    def clear(j, carry):
        flags[j] = -1
        return carry

    lax.fori_loop(0, blocks, clear, 0)

    def value_copy(j, t):
        return pltpu.make_async_copy(
            vals_hbm.at[t], vals.at[:, pl.ds(pl.multiple_of(j * 128, 128), 128)], val_sems.at[j])

    def find(t, carry):
        j = index_ref[t] - me * blocks

        @pl.when((j >= 0) & (j < blocks))
        def _():
            flags[j] = t
            value_copy(j, t).start()

        return carry

    lax.fori_loop(0, index_ref.shape[0], find, 0)

    def blank(j, carry):
        @pl.when(flags[j] < 0)
        def _():
            vals[:, pl.ds(pl.multiple_of(j * 128, 128), 128)] = jnp.zeros((vals.shape[0], 128), BF16)

        return carry

    lax.fori_loop(0, blocks, blank, 0)

    examples = acts.shape[0]
    rows = lax.broadcasted_iota(jnp.int32, (examples, examples), 0)
    order = jnp.where(rows == assign_ref[...], 1.0, 0.0).astype(BF16)
    copies[0].wait()
    copies[1].wait()
    in_part = nt_dot(proj[...], acts[...]).astype(BF16)
    in_part = jnp.dot(in_part, order, preferred_element_type=F32)

    def settle(j, carry):
        @pl.when(flags[j] >= 0)
        def _():
            value_copy(j, flags[j]).wait()

        return carry

    lax.fori_loop(0, blocks, settle, 0)
    copies[2].wait()
    out_part = nt_dot(vals[...], grads[...]).astype(BF16)
    out_part = jnp.dot(out_part, order, preferred_element_type=F32)
    for c in range(send_ref.shape[0]):
        send_ref[c, 0:64, :] = out_part[:, 0:128].astype(BF16)
        send_ref[c, 64:128, :] = out_part[:, 128:256].astype(BF16)
        tops = jnp.concatenate([in_part[8 * c:8 * c + 8, 0:128], in_part[8 * c:8 * c + 8, 128:256]], axis=0)
        send_ref[c, 128:144, :] = tops.astype(BF16)
        mine = jnp.concatenate(
            [in_part[16 * k:16 * k + 16, 32 * c:32 * c + 32] for k in range(4)], axis=1)
        send_ref[c, 144:160, :] = mine.astype(BF16)


TILES = [(i, j) for i in range(4) for j in range(i, 4)]


def gram_kernel(recv_ref, coords_ref, keep_ref, give_ref, ft, packed):
    total = recv_ref[0].astype(F32)
    for c in range(1, recv_ref.shape[0]):
        total = total + recv_ref[c].astype(F32)
    coords = total.astype(BF16)
    coords_ref[...] = coords
    wide = coords.astype(F32)
    out_t = (wide[0:64], wide[64:128])
    in_t = (wide[128:136], wide[136:144])
    for p in range(8):
        for h in range(2):
            ft[64 * p:64 * p + 64, 128 * h:128 * h + 128] = (in_t[h][p:p + 1] * out_t[h]).astype(BF16)
    for at, (i, j) in enumerate(TILES):
        packed[128 * at:128 * at + 128, :] = nt_dot(
            ft[128 * i:128 * i + 128, :], ft[128 * j:128 * j + 128, :]).astype(BF16)
    core = lax.rem(lax.axis_index("dp"), 2)
    half = packed.shape[0] // 2
    keep_ref[...] = packed[pl.ds(pl.multiple_of(core * half, half), half), :]
    give_ref[...] = packed[pl.ds(pl.multiple_of((1 - core) * half, half), half), :]


def features_kernel(coords_ref, features_ref):
    me = lax.axis_index("mp")
    coords = coords_ref[...]
    picked = jnp.concatenate([coords[0:64], coords[64:128]], axis=1)
    rows = lax.broadcasted_iota(jnp.int32, (32, 256), 0)
    cols = lax.broadcasted_iota(jnp.int32, (32, 256), 1)
    pick = jnp.where(cols == rows + 32 * me, 1.0, 0.0).astype(BF16)
    outs = nt_dot(pick, picked)
    wide = coords[144:160].astype(F32)
    mine = jnp.concatenate([wide[:, 32 * k:32 * k + 32] for k in range(4)], axis=0).astype(BF16)
    turn = jnp.where(
        lax.broadcasted_iota(jnp.int32, (32, 32), 0) == lax.broadcasted_iota(jnp.int32, (32, 32), 1),
        1.0, 0.0).astype(BF16)
    ins = nt_dot(turn, mine).astype(BF16)
    both = jnp.concatenate([outs, outs], axis=1)
    step = 512
    for at in range(features_ref.shape[1] // step):
        p = lax.broadcasted_iota(jnp.int32, (64, step), 0)
        f = lax.broadcasted_iota(jnp.int32, (64, step), 1)
        spread = jnp.where(p == (step // 64) * at + lax.div(f, 64), 1.0, 0.0).astype(BF16)
        left = jnp.dot(ins, spread, preferred_element_type=F32)
        for w in range(step // 128):
            features_ref[:, step * at + 128 * w:step * at + 128 * w + 128] = (
                left[:, 128 * w:128 * w + 128] * both).astype(BF16)


def spread_lane(x, at):
    return jnp.take_along_axis(x, jnp.full((8, 128), at, jnp.int32), axis=1)

def row(x, j):
    return jnp.broadcast_to(x[j:j + 1, :], (8, 128))

WIDE = 16


def factor_block(c):
    sub = lax.broadcasted_iota(jnp.int32, (8, 128), 0)
    lane = lax.broadcasted_iota(jnp.int32, (8, 128), 1)
    n = len(c)
    h = WIDE // 8
    upper, inverse = [], []
    for p in range(0, n, h):
        base = 8 * p
        inside = (lane >= base) & (lane < base + WIDE)
        own = [c[p + u] for u in range(h)]
        cols = [[spread_lane(own[u], base + k) for u in range(h)] for k in range(WIDE)]
        if p:
            cols[0][0] = cols[0][0] + 0.0 * (cols[WIDE - 1][h - 1] + cols[WIDE - 2][h - 1])
        aug = [jnp.where(inside, jnp.where(lane - base == sub + 8 * u, 1.0, 0.0), own[u]) for u in range(h)]
        zed = list(aug)
        near = range(p + h, min(p + 2 * h, n))
        below = {t: [spread_lane(c[t], base + k) for k in range(WIDE)] for t in near}
        inv = [jnp.zeros((8, 128), F32) for _ in range(h)]
        for j in range(WIDE):
            v, i = divmod(j, 8)
            r = 1.0 / row(cols[j][v], i)
            inv[v] = jnp.where(sub == i, r, inv[v])
            full = [jnp.where(sub == i, 0.0, cols[j][u]) if u == v else cols[j][u] for u in range(h)]
            m = [x * r for x in full]
            part = jnp.where(sub > i, m[v], 0.0)
            for k in range(j + 1, WIDE):
                s = row(cols[k][v], i)
                for u in range(h):
                    if k == j + 1:
                        cols[k][u] = cols[k][u] - (full[u] * s) * r
                    else:
                        cols[k][u] = cols[k][u] - m[u] * s
            ro, ra, rz = row(own[v], i), row(aug[v], i), row(zed[v], i)
            for u in range(h):
                if u >= v:
                    low = part if u == v else m[u]
                    own[u] = own[u] - low * ro
                    aug[u] = aug[u] - low * ra
                zed[u] = zed[u] - m[u] * rz
        rows, dones = [], []
        for u in range(h):
            root = jnp.sqrt(inv[u])
            at = base + 8 * u
            upper.append(jnp.where(lane >= at + sub, own[u] * root, 0.0))
            inverse.append(jnp.where(lane <= at + sub, aug[u] * root, 0.0))
            done = zed[u] * inv[u]
            dones.append(done)
            rows += [row(done, k) for k in range(8)]
        for t in near:
            s = [below[t][k] * rows[k] for k in range(WIDE)]
            while len(s) > 1:
                s = [s[k] + s[k + 1] for k in range(0, len(s), 2)]
            c[t] = jnp.where(inside, 0.0, c[t]) - s[0]
        far = range(p + 2 * h, n)
        if far:
            pad = [jnp.zeros((8, 128), F32)] * n
            for u in range(h):
                pad[p + u] = dones[u]
            change = jnp.dot(jnp.concatenate([c[t] for t in far], axis=0), jnp.concatenate(pad, axis=0),
                             preferred_element_type=F32, precision=lax.Precision.HIGHEST)
            for at, t in enumerate(far):
                c[t] = jnp.where(inside, 0.0, c[t]) - change[8 * at:8 * at + 8]
    return upper, inverse


def factor_kernel(total_ref, other_ref, out_ref, work, inv):
    core = lax.rem(lax.axis_index("dp"), 2)
    half = total_ref.shape[0]
    at0 = pl.multiple_of(core * half, half); at1 = pl.multiple_of((1 - core) * half, half)
    work[pl.ds(at0, half), :] = total_ref[...].astype(F32) * (1.0 / 8192)
    work[pl.ds(at1, half), :] = other_ref[...].astype(F32) * (1.0 / 8192)
    place = {ij: 128 * n for n, ij in enumerate(TILES)}
    sub = lax.broadcasted_iota(jnp.int32, (8, 128), 0)
    lane = lax.broadcasted_iota(jnp.int32, (8, 128), 1)
    for s in range(4):
        o = place[s, s]
        c = [work[o + 8 * t:o + 8 * t + 8, :] + jnp.where(lane == sub + 8 * t, DAMPING, 0.0) for t in range(16)]
        upper, inverse = factor_block(c)
        for t in range(16):
            out_ref[128 * s + 8 * t:128 * s + 8 * t + 8, 128 * s:128 * s + 128] = upper[t]
            inv[8 * t:8 * t + 8, :] = inverse[t]
        for j in range(s):
            out_ref[128 * s:128 * s + 128, 128 * j:128 * j + 128] = jnp.zeros((128, 128), F32)
        for j in range(s + 1, 4):
            a = work[place[s, j]:place[s, j] + 128, :]
            out_ref[128 * s:128 * s + 128, 128 * j:128 * j + 128] = jnp.dot(
                inv[...], a, preferred_element_type=F32, precision=lax.Precision.HIGHEST)
        for i in range(s + 1, 4):
            for j in range(i, 4):
                ri = out_ref[128 * s:128 * s + 128, 128 * i:128 * i + 128]
                rj = out_ref[128 * s:128 * s + 128, 128 * j:128 * j + 128]
                work[place[i, j]:place[i, j] + 128, :] -= lax.dot_general(
                    ri, rj, (((0,), (0,)), ((), ())), preferred_element_type=F32, precision=lax.Precision.HIGHEST)

def spot(y, x, core):
    return (y * 4 + x) * 2 + core


def moves(step):
    return [(spot(y, x, c), spot(*step(y, x, c)))
            for y in range(4) for x in range(4) for c in range(2)]


def shards(acts, grads, proj_in, block_vals, block_index, assign):
    ex, k_in = acts.shape
    k_out = grads.shape[1]
    any_spec = pl.BlockSpec(memory_space=pl.ANY)
    vmem = pl.BlockSpec(memory_space=pltpu.VMEM)
    smem = pl.BlockSpec(memory_space=pltpu.SMEM)
    send = pl.pallas_call(
        project_kernel,
        out_shape=jax.ShapeDtypeStruct((8, 160, 128), BF16),
        in_specs=[smem, vmem, any_spec, any_spec, any_spec, any_spec],
        out_specs=vmem,
        scratch_shapes=[
            pltpu.VMEM((ex, k_in), BF16),
            pltpu.VMEM((ex, k_out), BF16),
            pltpu.VMEM((64, k_in), BF16),
            pltpu.VMEM((64, k_out), BF16),
            pltpu.SMEM((k_out // 128,), jnp.int32),
            pltpu.SemaphoreType.DMA((3,)),
            pltpu.SemaphoreType.DMA((k_out // 128,)),
        ],
        name="project",
    )(block_index, assign, acts, grads, proj_in.T, jnp.swapaxes(block_vals, 1, 2))
    recv = lax.all_to_all(send, "mp", 0, 0, tiled=True)
    coords, keep, give = pl.pallas_call(
        gram_kernel,
        out_shape=(
            jax.ShapeDtypeStruct((160, 128), BF16),
            jax.ShapeDtypeStruct((640, 128), BF16),
            jax.ShapeDtypeStruct((640, 128), BF16),
        ),
        in_specs=[vmem],
        out_specs=(vmem, vmem, vmem),
        scratch_shapes=[pltpu.VMEM((FB, 256), BF16), pltpu.VMEM((1280, 128), BF16)],
        compiler_params=pltpu.CompilerParams(vmem_limit_bytes=12 << 20),
        name="gram",
    )(recv)
    features = pl.pallas_call(
        features_kernel,
        out_shape=jax.ShapeDtypeStruct((32, 4096), BF16),
        in_specs=[vmem],
        out_specs=vmem,
        cost_estimate=pl.CostEstimate(flops=2 * 32 * 64 * 4096, bytes_accessed=300000, transcendentals=0),
        compiler_params=pltpu.CompilerParams(vmem_limit_bytes=12 << 20),
        name="features",
    )(coords)
    total = keep + lax.ppermute(give, "dp", moves(lambda y, x, c: (y, x, 1 - c)))
    for step in (
        lambda y, x, c: (y, x ^ 1, c),
        lambda y, x, c: (y, 3 - x, c),
        lambda y, x, c: (y ^ 1, x, c),
        lambda y, x, c: (3 - y, x, c),
    ):
        total = total + lax.ppermute(total, "dp", moves(step))
        total, features = lax.optimization_barrier((total, features))
    other = lax.ppermute(total, "dp", moves(lambda y, x, c: (y, x, 1 - c)))
    factor = pl.pallas_call(
        factor_kernel,
        out_shape=jax.ShapeDtypeStruct((FB, FB), F32),
        in_specs=[vmem, vmem],
        out_specs=vmem,
        scratch_shapes=[pltpu.VMEM((1280, 128), F32), pltpu.VMEM((128, 128), F32)],
        compiler_params=pltpu.CompilerParams(vmem_limit_bytes=12 << 20),
        name="factor",
    )(total, other).reshape(1, FB, FB)
    return features, factor


def solution(mesh):
    return jax.shard_map(
        shards,
        mesh=mesh,
        in_specs=(P("dp", "mp"), P("dp", "mp"), P(), P(), P(), P("dp", None)),
        out_specs=(P(("dp", "mp"), None), P("mp", None, None)),
        check_vma=False,
    )
```

```python
import functools

import jax
import jax.numpy as jnp
from jax import lax
from jax.experimental import pallas as pl
from jax.experimental.pallas import tpu as pltpu
from jax.sharding import PartitionSpec as P

FB = 512
DAMPING = 0.05
BF16 = jnp.bfloat16
F32 = jnp.float32
NT = (((1,), (1,)), ((), ()))


def nt_dot(a, b):
    return lax.dot_general(a, b, NT, preferred_element_type=F32)


def project_kernel(index_hbm, assign_hbm, acts_hbm, grads_hbm, proj_hbm, vals_hbm, send_ref,
                   index, assign, acts, grads, proj, vals, flags, sems, val_sems):
    me = lax.axis_index("mp")
    k_in = acts.shape[1]
    k_half = grads.shape[1] // 2
    blocks = val_sems.shape[0]
    in_copies = (
        pltpu.make_async_copy(index_hbm, index, sems.at[0]),
        pltpu.make_async_copy(proj_hbm.at[:, pl.ds(pl.multiple_of(me * k_in, 128), k_in)], proj, sems.at[1]),
        pltpu.make_async_copy(acts_hbm, acts, sems.at[2]),
        pltpu.make_async_copy(assign_hbm, assign, sems.at[3]),
    )
    out_copies = [
        pltpu.make_async_copy(grads_hbm.at[:, k_half * n:k_half * n + k_half],
                              grads.at[:, k_half * n:k_half * n + k_half], sems.at[4 + n])
        for n in range(2)
    ]
    for copy in (*in_copies, *out_copies):
        copy.start()
    vals[...] = jnp.zeros(vals.shape, BF16)
    for j in range(blocks):
        flags[j] = -1
    in_copies[0].wait()

    def value_copy(j, t):
        return pltpu.make_async_copy(
            vals_hbm.at[t], vals.at[:, pl.ds(pl.multiple_of(j * 128, 128), 128)], val_sems.at[j])

    def find(t, carry):
        j = index[t] - me * blocks

        @pl.when((j >= 0) & (j < blocks))
        def _():
            flags[j] = t
            value_copy(j, t).start()

        return carry

    lax.fori_loop(0, index.shape[0], find, 0, unroll=16)

    examples = acts.shape[0]
    in_copies[3].wait()
    rows = lax.broadcasted_iota(jnp.int32, (examples, examples), 0)
    order = jnp.where(rows == assign[...], 1.0, 0.0).astype(BF16)
    in_copies[1].wait()
    in_copies[2].wait()
    in_part = nt_dot(proj[...], acts[...]).astype(BF16)
    in_part = jnp.dot(in_part, order, preferred_element_type=F32)

    def settle(j, carry):
        @pl.when(flags[j] >= 0)
        def _():
            value_copy(j, flags[j]).wait()

        return carry

    lax.fori_loop(0, blocks, settle, 0, unroll=4)
    out_copies[0].wait()
    out_part = nt_dot(vals[:, 0:k_half], grads[:, 0:k_half])
    out_copies[1].wait()
    out_part = out_part + nt_dot(vals[:, k_half:2 * k_half], grads[:, k_half:2 * k_half])
    out_part = jnp.dot(out_part.astype(BF16), order, preferred_element_type=F32)
    for c in range(send_ref.shape[0]):
        send_ref[c, 0:64, :] = out_part[:, 0:128].astype(BF16)
        send_ref[c, 64:128, :] = out_part[:, 128:256].astype(BF16)
        tops = jnp.concatenate([in_part[8 * c:8 * c + 8, 0:128], in_part[8 * c:8 * c + 8, 128:256]], axis=0)
        send_ref[c, 128:144, :] = tops.astype(BF16)
        mine = jnp.concatenate(
            [in_part[16 * k:16 * k + 16, 32 * c:32 * c + 32] for k in range(4)], axis=1)
        send_ref[c, 144:160, :] = mine.astype(BF16)


TILES = [(i, j) for i in range(4) for j in range(i, 4)]
HALF = 336


def gram_kernel(recv_ref, coords_ref, keep_ref, give_ref, ft, packed):
    total = recv_ref[0].astype(F32)
    for c in range(1, recv_ref.shape[0]):
        total = total + recv_ref[c].astype(F32)
    coords = total.astype(BF16)
    coords_ref[...] = coords
    wide = coords.astype(F32)
    out_t = (wide[0:64], wide[64:128])
    in_t = (wide[128:136], wide[136:144])
    for p in range(8):
        for h in range(2):
            ft[64 * p:64 * p + 64, 128 * h:128 * h + 128] = (in_t[h][p:p + 1] * out_t[h]).astype(BF16)
    row32 = lax.broadcasted_iota(jnp.int32, (32, 128), 0)
    lane64 = lax.rem(lax.broadcasted_iota(jnp.int32, (32, 128), 1), 64)
    from_low = (lane64 < 32) & (row32 > lane64)
    on_diagonal = lane64 == row32 + 32
    left = lax.broadcasted_iota(jnp.int32, (32, 128), 1) < 64
    for half in range(2):
        spare = []
        for at, (i, j) in enumerate(TILES[5 * half:5 * half + 5]):
            tile = nt_dot(ft[128 * i:128 * i + 128, :], ft[128 * j:128 * j + 128, :])
            for u in range(2):
                top, low = tile[64 * u:64 * u + 32], tile[64 * u + 32:64 * u + 64]
                one = jnp.where(from_low, pltpu.roll(low, 96, 1), top)
                last = jnp.sum(jnp.where(on_diagonal, low, 0.0), axis=0, keepdims=True)
                if i == j and u == 0:
                    first = (one, last)
                elif i == j:
                    one = jnp.where(left, pltpu.roll(first[0], 64, 1), one)
                    last = jnp.where(left[0:1], pltpu.roll(first[1], 64, 1), last)
                packed[HALF * half + 64 * at + 32 * u:HALF * half + 64 * at + 32 * u + 32, :] = one.astype(BF16)
                spare.append(last)
        spare.append(jnp.zeros((6, 128), F32))
        packed[HALF * half + 320:HALF * half + 336, :] = jnp.concatenate(spare, axis=0).astype(BF16)
    core = lax.rem(lax.axis_index("dp"), 2)
    keep_ref[...] = packed[pl.ds(pl.multiple_of(core * HALF, HALF), HALF), :]
    give_ref[...] = packed[pl.ds(pl.multiple_of((1 - core) * HALF, HALF), HALF), :]


def features_kernel(coords_ref, features_ref):
    me = lax.axis_index("mp")
    coords = coords_ref[...]
    picked = jnp.concatenate([coords[0:64], coords[64:128]], axis=1)
    rows = lax.broadcasted_iota(jnp.int32, (32, 256), 0)
    cols = lax.broadcasted_iota(jnp.int32, (32, 256), 1)
    pick = jnp.where(cols == rows + 32 * me, 1.0, 0.0).astype(BF16)
    outs = nt_dot(pick, picked)
    wide = coords[144:160].astype(F32)
    mine = jnp.concatenate([wide[:, 32 * k:32 * k + 32] for k in range(4)], axis=0).astype(BF16)
    turn = jnp.where(
        lax.broadcasted_iota(jnp.int32, (32, 32), 0) == lax.broadcasted_iota(jnp.int32, (32, 32), 1),
        1.0, 0.0).astype(BF16)
    ins = nt_dot(turn, mine).astype(BF16)
    both = jnp.concatenate([outs, outs], axis=1)
    step = 512
    for at in range(features_ref.shape[1] // step):
        p = lax.broadcasted_iota(jnp.int32, (64, step), 0)
        f = lax.broadcasted_iota(jnp.int32, (64, step), 1)
        spread = jnp.where(p == (step // 64) * at + lax.div(f, 64), 1.0, 0.0).astype(BF16)
        left = jnp.dot(ins, spread, preferred_element_type=F32)
        for w in range(step // 128):
            features_ref[:, step * at + 128 * w:step * at + 128 * w + 128] = (
                left[:, 128 * w:128 * w + 128] * both).astype(BF16)


def spread_lane(x, at):
    return jnp.take_along_axis(x, jnp.full((8, 128), at, jnp.int32), axis=1)

def row(x, j):
    return jnp.broadcast_to(x[j:j + 1, :], (8, 128))

WIDE = 16


def factor_block(c):
    sub = lax.broadcasted_iota(jnp.int32, (8, 128), 0)
    lane = lax.broadcasted_iota(jnp.int32, (8, 128), 1)
    n = len(c)
    h = WIDE // 8
    upper, inverse = [], []
    for p in range(0, n, h):
        base = 8 * p
        inside = (lane >= base) & (lane < base + WIDE)
        own = [c[p + u] for u in range(h)]
        cols = [[spread_lane(own[u], base + k) for u in range(h)] for k in range(WIDE)]
        if p:
            cols[0][0] = cols[0][0] + 0.0 * (cols[WIDE - 1][h - 1] + cols[WIDE - 2][h - 1])
        aug = [jnp.where(inside, jnp.where(lane - base == sub + 8 * u, 1.0, 0.0), own[u]) for u in range(h)]
        zed = list(aug)
        near = range(p + h, min(p + 2 * h, n))
        below = {t: [spread_lane(c[t], base + k) for k in range(WIDE)] for t in near}
        inv = [jnp.zeros((8, 128), F32) for _ in range(h)]
        for j in range(WIDE):
            v, i = divmod(j, 8)
            r = 1.0 / row(cols[j][v], i)
            inv[v] = jnp.where(sub == i, r, inv[v])
            full = [jnp.where(sub == i, 0.0, cols[j][u]) if u == v else cols[j][u] for u in range(h)]
            m = [x * r for x in full]
            part = jnp.where(sub > i, m[v], 0.0)
            for k in range(j + 1, WIDE):
                s = row(cols[k][v], i)
                for u in range(h):
                    if k == j + 1:
                        cols[k][u] = cols[k][u] - (full[u] * s) * r
                    else:
                        cols[k][u] = cols[k][u] - m[u] * s
            ro, ra, rz = row(own[v], i), row(aug[v], i), row(zed[v], i)
            for u in range(h):
                if u >= v:
                    low = part if u == v else m[u]
                    own[u] = own[u] - low * ro
                    aug[u] = aug[u] - low * ra
                zed[u] = zed[u] - m[u] * rz
        rows, dones = [], []
        for u in range(h):
            root = jnp.sqrt(inv[u])
            at = base + 8 * u
            upper.append(jnp.where(lane >= at + sub, own[u] * root, 0.0))
            inverse.append(jnp.where(lane <= at + sub, aug[u] * root, 0.0))
            done = zed[u] * inv[u]
            dones.append(done)
            rows += [row(done, k) for k in range(8)]
        for t in near:
            s = [below[t][k] * rows[k] for k in range(WIDE)]
            while len(s) > 1:
                s = [s[k] + s[k + 1] for k in range(0, len(s), 2)]
            c[t] = jnp.where(inside, 0.0, c[t]) - s[0]
        far = range(p + 2 * h, n)
        if far:
            pad = [jnp.zeros((8, 128), F32)] * n
            for u in range(h):
                pad[p + u] = dones[u]
            change = jnp.dot(jnp.concatenate([c[t] for t in far], axis=0), jnp.concatenate(pad, axis=0),
                             preferred_element_type=F32, precision=lax.Precision.HIGHEST)
            for at, t in enumerate(far):
                c[t] = jnp.where(inside, 0.0, c[t]) - change[8 * at:8 * at + 8]
    return upper, inverse


def factor_kernel(total_ref, other_ref, out_ref, packed, work, inv):
    core = lax.rem(lax.axis_index("dp"), 2)
    packed[pl.ds(pl.multiple_of(core * HALF, HALF), HALF), :] = total_ref[...]
    packed[pl.ds(pl.multiple_of((1 - core) * HALF, HALF), HALF), :] = other_ref[...]
    unit = jnp.where(
        lax.broadcasted_iota(jnp.int32, (128, 128), 0) == lax.broadcasted_iota(jnp.int32, (128, 128), 1),
        1.0, 0.0).astype(BF16)
    row32 = lax.broadcasted_iota(jnp.int32, (32, 128), 0)
    lane128 = lax.broadcasted_iota(jnp.int32, (32, 128), 1)
    lane64 = lax.rem(lane128, 64)
    left = lane128 < 64
    outer = lane64 < 32
    for at in range(10):
        half, spot_in = divmod(at, 5)
        for u in range(2):
            base = HALF * half + 64 * spot_in + 32 * u
            raw = packed[base:base + 32, :]
            turned = nt_dot(unit, jnp.concatenate([raw] * 4, axis=0))
            wide = raw.astype(F32)
            spare = packed[HALF * half + 320:HALF * half + 336, :].astype(F32)[2 * spot_in + u:2 * spot_in + u + 1]
            own = jnp.where(left, turned[0:32], turned[64:96])
            cross = jnp.where(left, turned[32:64], turned[96:128])
            top = jnp.where(outer & (row32 > lane64), own, wide)
            low = jnp.where(row32 > lane64 - 32, pltpu.roll(wide, 32, 1), own)
            low = jnp.where(row32 == lane64 - 32, spare, low)
            low = jnp.where(outer, cross, low)
            work[128 * at + 64 * u:128 * at + 64 * u + 32, :] = top * (1.0 / 8192)
            work[128 * at + 64 * u + 32:128 * at + 64 * u + 64, :] = low * (1.0 / 8192)
    place = {ij: 128 * n for n, ij in enumerate(TILES)}
    sub = lax.broadcasted_iota(jnp.int32, (8, 128), 0)
    lane = lax.broadcasted_iota(jnp.int32, (8, 128), 1)
    for s in range(4):
        o = place[s, s]
        c = [work[o + 8 * t:o + 8 * t + 8, :] + jnp.where(lane == sub + 8 * t, DAMPING, 0.0) for t in range(16)]
        upper, inverse = factor_block(c)
        for t in range(16):
            out_ref[128 * s + 8 * t:128 * s + 8 * t + 8, 128 * s:128 * s + 128] = upper[t]
            inv[8 * t:8 * t + 8, :] = inverse[t]
        for j in range(s):
            out_ref[128 * s:128 * s + 128, 128 * j:128 * j + 128] = jnp.zeros((128, 128), F32)
        for j in range(s + 1, 4):
            a = work[place[s, j]:place[s, j] + 128, :]
            out_ref[128 * s:128 * s + 128, 128 * j:128 * j + 128] = jnp.dot(
                inv[...], a, preferred_element_type=F32, precision=lax.Precision.HIGHEST)
        for i in range(s + 1, 4):
            for j in range(i, 4):
                ri = out_ref[128 * s:128 * s + 128, 128 * i:128 * i + 128]
                rj = out_ref[128 * s:128 * s + 128, 128 * j:128 * j + 128]
                work[place[i, j]:place[i, j] + 128, :] -= lax.dot_general(
                    ri, rj, (((0,), (0,)), ((), ())), preferred_element_type=F32, precision=lax.Precision.HIGHEST)

def spot(y, x, core):
    return (y * 4 + x) * 2 + core


def moves(step):
    return [(spot(y, x, c), spot(*step(y, x, c)))
            for y in range(4) for x in range(4) for c in range(2)]


def shards(acts, grads, proj_in, block_vals, block_index, assign):
    ex, k_in = acts.shape
    k_out = grads.shape[1]
    hbm = pl.BlockSpec(memory_space=pltpu.HBM)
    vmem = pl.BlockSpec(memory_space=pltpu.VMEM)
    send = pl.pallas_call(
        project_kernel,
        out_shape=jax.ShapeDtypeStruct((8, 160, 128), BF16),
        in_specs=[hbm] * 6,
        out_specs=vmem,
        scratch_shapes=[
            pltpu.SMEM((block_index.shape[0],), jnp.int32),
            pltpu.VMEM((1, ex), jnp.int32),
            pltpu.VMEM((ex, k_in), BF16),
            pltpu.VMEM((ex, k_out), BF16),
            pltpu.VMEM((64, k_in), BF16),
            pltpu.VMEM((64, k_out), BF16),
            pltpu.SMEM((k_out // 128,), jnp.int32),
            pltpu.SemaphoreType.DMA((6,)),
            pltpu.SemaphoreType.DMA((k_out // 128,)),
        ],
        compiler_params=pltpu.CompilerParams(vmem_limit_bytes=16 << 20),
        name="project",
    )(*(pltpu.with_memory_space_constraint(x, pltpu.HBM) for x in (
        block_index, assign, acts, grads, proj_in.T, jnp.swapaxes(block_vals, 1, 2))))
    recv = lax.all_to_all(send, "mp", 0, 0, tiled=True)
    coords, keep, give = pl.pallas_call(
        gram_kernel,
        out_shape=(
            jax.ShapeDtypeStruct((160, 128), BF16),
            jax.ShapeDtypeStruct((HALF, 128), BF16),
            jax.ShapeDtypeStruct((HALF, 128), BF16),
        ),
        in_specs=[vmem],
        out_specs=(vmem, vmem, vmem),
        scratch_shapes=[pltpu.VMEM((FB, 256), BF16), pltpu.VMEM((2 * HALF, 128), BF16)],
        compiler_params=pltpu.CompilerParams(vmem_limit_bytes=12 << 20),
        name="gram",
    )(recv)
    features = pl.pallas_call(
        features_kernel,
        out_shape=jax.ShapeDtypeStruct((32, 4096), BF16),
        in_specs=[vmem],
        out_specs=vmem,
        cost_estimate=pl.CostEstimate(flops=2 * 32 * 64 * 4096, bytes_accessed=300000, transcendentals=0),
        compiler_params=pltpu.CompilerParams(vmem_limit_bytes=12 << 20),
        name="features",
    )(coords)
    total = keep + lax.ppermute(give, "dp", moves(lambda y, x, c: (y, x, 1 - c)))
    for step in (
        lambda y, x, c: (y, x ^ 1, c),
        lambda y, x, c: (y, 3 - x, c),
        lambda y, x, c: (y ^ 1, x, c),
        lambda y, x, c: (3 - y, x, c),
    ):
        total = total + lax.ppermute(total, "dp", moves(step))
        total, features = lax.optimization_barrier((total, features))
    other = lax.ppermute(total, "dp", moves(lambda y, x, c: (y, x, 1 - c)))
    factor = pl.pallas_call(
        factor_kernel,
        out_shape=jax.ShapeDtypeStruct((FB, FB), F32),
        in_specs=[vmem, vmem],
        out_specs=vmem,
        scratch_shapes=[pltpu.VMEM((2 * HALF, 128), BF16), pltpu.VMEM((1280, 128), F32), pltpu.VMEM((128, 128), F32)],
        compiler_params=pltpu.CompilerParams(vmem_limit_bytes=12 << 20),
        name="factor",
    )(total, other).reshape(1, FB, FB)
    return features, factor


def solution(mesh):
    return jax.shard_map(
        shards,
        mesh=mesh,
        in_specs=(P("dp", "mp"), P("dp", "mp"), P(), P(), P(), P("dp", None)),
        out_specs=(P(("dp", "mp"), None), P("mp", None, None)),
        check_vma=False,
    )
```

```python
import functools

import jax
import jax.numpy as jnp
from jax import lax
from jax.experimental import pallas as pl
from jax.experimental.pallas import tpu as pltpu
from jax.sharding import PartitionSpec as P

FB = 512
DAMPING = 0.05
BF16 = jnp.bfloat16
F32 = jnp.float32
NT = (((1,), (1,)), ((), ()))


def nt_dot(a, b):
    return lax.dot_general(a, b, NT, preferred_element_type=F32)


def project_kernel(index_hbm, assign_hbm, acts_hbm, grads_hbm, proj_hbm, vals_hbm, send_ref,
                   index, assign, acts, grads, proj, vals, flags, sems, val_sems):
    me = lax.axis_index("mp")
    k_in = acts.shape[1]
    k_half = grads.shape[1] // 2
    blocks = val_sems.shape[0]
    in_copies = (
        pltpu.make_async_copy(index_hbm, index, sems.at[0]),
        pltpu.make_async_copy(proj_hbm.at[:, pl.ds(pl.multiple_of(me * k_in, 128), k_in)], proj, sems.at[1]),
        pltpu.make_async_copy(acts_hbm, acts, sems.at[2]),
        pltpu.make_async_copy(assign_hbm, assign, sems.at[3]),
    )
    out_copies = [
        pltpu.make_async_copy(grads_hbm.at[:, k_half * n:k_half * n + k_half],
                              grads.at[:, k_half * n:k_half * n + k_half], sems.at[4 + n])
        for n in range(2)
    ]
    for copy in (*in_copies, *out_copies):
        copy.start()
    vals[...] = jnp.zeros(vals.shape, BF16)
    for j in range(blocks):
        flags[j] = -1
    in_copies[0].wait()

    def value_copy(j, t):
        return pltpu.make_async_copy(
            vals_hbm.at[t], vals.at[:, pl.ds(pl.multiple_of(j * 128, 128), 128)], val_sems.at[j])

    def find(t, carry):
        j = index[t] - me * blocks

        @pl.when((j >= 0) & (j < blocks))
        def _():
            flags[j] = t
            value_copy(j, t).start()

        return carry

    lax.fori_loop(0, index.shape[0], find, 0, unroll=16)

    examples = acts.shape[0]
    in_copies[3].wait()
    rows = lax.broadcasted_iota(jnp.int32, (examples, examples), 0)
    order = jnp.where(rows == assign[...], 1.0, 0.0).astype(BF16)
    in_copies[1].wait()
    in_copies[2].wait()
    in_part = nt_dot(proj[...], acts[...]).astype(BF16)
    in_part = jnp.dot(in_part, order, preferred_element_type=F32)

    def settle(j, carry):
        @pl.when(flags[j] >= 0)
        def _():
            value_copy(j, flags[j]).wait()

        return carry

    lax.fori_loop(0, blocks, settle, 0, unroll=4)
    out_copies[0].wait()
    out_part = nt_dot(vals[:, 0:k_half], grads[:, 0:k_half])
    out_copies[1].wait()
    out_part = out_part + nt_dot(vals[:, k_half:2 * k_half], grads[:, k_half:2 * k_half])
    out_part = jnp.dot(out_part.astype(BF16), order, preferred_element_type=F32)
    for c in range(send_ref.shape[0]):
        send_ref[c, 0:64, :] = out_part[:, 0:128].astype(BF16)
        send_ref[c, 64:128, :] = out_part[:, 128:256].astype(BF16)
        tops = jnp.concatenate([in_part[8 * c:8 * c + 8, 0:128], in_part[8 * c:8 * c + 8, 128:256]], axis=0)
        send_ref[c, 128:144, :] = tops.astype(BF16)
        mine = jnp.concatenate(
            [in_part[16 * k:16 * k + 16, 32 * c:32 * c + 32] for k in range(4)], axis=1)
        send_ref[c, 144:160, :] = mine.astype(BF16)


TILES = [(i, j) for i in range(4) for j in range(i, 4)]
HALF = 336


def gram_kernel(recv_ref, coords_ref, keep_ref, give_ref, ft, packed):
    total = recv_ref[0].astype(F32)
    for c in range(1, recv_ref.shape[0]):
        total = total + recv_ref[c].astype(F32)
    coords = total.astype(BF16)
    coords_ref[...] = coords
    wide = coords.astype(F32)
    out_t = (wide[0:64], wide[64:128])
    in_t = (wide[128:136], wide[136:144])
    for p in range(8):
        for h in range(2):
            ft[64 * p:64 * p + 64, 128 * h:128 * h + 128] = (in_t[h][p:p + 1] * out_t[h]).astype(BF16)
    row32 = lax.broadcasted_iota(jnp.int32, (32, 128), 0)
    lane64 = lax.rem(lax.broadcasted_iota(jnp.int32, (32, 128), 1), 64)
    from_low = (lane64 < 32) & (row32 > lane64)
    on_diagonal = lane64 == row32 + 32
    left = lax.broadcasted_iota(jnp.int32, (32, 128), 1) < 64
    for half in range(2):
        spare = []
        for at, (i, j) in enumerate(TILES[5 * half:5 * half + 5]):
            tile = nt_dot(ft[128 * i:128 * i + 128, :], ft[128 * j:128 * j + 128, :])
            for u in range(2):
                top, low = tile[64 * u:64 * u + 32], tile[64 * u + 32:64 * u + 64]
                one = jnp.where(from_low, pltpu.roll(low, 96, 1), top)
                last = jnp.sum(jnp.where(on_diagonal, low, 0.0), axis=0, keepdims=True)
                if i == j and u == 0:
                    first = (one, last)
                elif i == j:
                    one = jnp.where(left, pltpu.roll(first[0], 64, 1), one)
                    last = jnp.where(left[0:1], pltpu.roll(first[1], 64, 1), last)
                packed[HALF * half + 64 * at + 32 * u:HALF * half + 64 * at + 32 * u + 32, :] = one.astype(BF16)
                spare.append(last)
        spare.append(jnp.zeros((6, 128), F32))
        packed[HALF * half + 320:HALF * half + 336, :] = jnp.concatenate(spare, axis=0).astype(BF16)
    core = lax.rem(lax.axis_index("dp"), 2)
    keep_ref[...] = packed[pl.ds(pl.multiple_of(core * HALF, HALF), HALF), :]
    give_ref[...] = packed[pl.ds(pl.multiple_of((1 - core) * HALF, HALF), HALF), :]


def features_kernel(coords_ref, features_ref):
    me = lax.axis_index("mp")
    coords = coords_ref[...]
    picked = jnp.concatenate([coords[0:64], coords[64:128]], axis=1)
    rows = lax.broadcasted_iota(jnp.int32, (32, 256), 0)
    cols = lax.broadcasted_iota(jnp.int32, (32, 256), 1)
    pick = jnp.where(cols == rows + 32 * me, 1.0, 0.0).astype(BF16)
    outs = nt_dot(pick, picked)
    wide = coords[144:160].astype(F32)
    mine = jnp.concatenate([wide[:, 32 * k:32 * k + 32] for k in range(4)], axis=0).astype(BF16)
    turn = jnp.where(
        lax.broadcasted_iota(jnp.int32, (32, 32), 0) == lax.broadcasted_iota(jnp.int32, (32, 32), 1),
        1.0, 0.0).astype(BF16)
    ins = nt_dot(turn, mine).astype(BF16)
    both = jnp.concatenate([outs, outs], axis=1)
    step = 512
    for at in range(features_ref.shape[1] // step):
        p = lax.broadcasted_iota(jnp.int32, (64, step), 0)
        f = lax.broadcasted_iota(jnp.int32, (64, step), 1)
        spread = jnp.where(p == (step // 64) * at + lax.div(f, 64), 1.0, 0.0).astype(BF16)
        left = jnp.dot(ins, spread, preferred_element_type=F32)
        for w in range(step // 128):
            features_ref[:, step * at + 128 * w:step * at + 128 * w + 128] = (
                left[:, 128 * w:128 * w + 128] * both).astype(BF16)


def spread_lane(x, at):
    return jnp.take_along_axis(x, jnp.full((8, 128), at, jnp.int32), axis=1)

def row(x, j):
    return jnp.broadcast_to(x[j:j + 1, :], (8, 128))

WIDE = 16


def factor_block(c):
    sub = lax.broadcasted_iota(jnp.int32, (8, 128), 0)
    lane = lax.broadcasted_iota(jnp.int32, (8, 128), 1)
    n = len(c)
    h = WIDE // 8
    upper, inverse = [], []
    for p in range(0, n, h):
        base = 8 * p
        inside = (lane >= base) & (lane < base + WIDE)
        own = [c[p + u] for u in range(h)]
        cols = [[spread_lane(own[u], base + k) for u in range(h)] for k in range(WIDE)]
        if p:
            cols[0][0] = cols[0][0] + 0.0 * (cols[WIDE - 1][h - 1] + cols[WIDE - 2][h - 1])
        aug = [jnp.where(inside, jnp.where(lane - base == sub + 8 * u, 1.0, 0.0), own[u]) for u in range(h)]
        zed = list(aug)
        near = range(p + h, min(p + 2 * h, n))
        below = {t: [spread_lane(c[t], base + k) for k in range(WIDE)] for t in near}
        inv = [jnp.zeros((8, 128), F32) for _ in range(h)]
        for j in range(WIDE):
            v, i = divmod(j, 8)
            r = 1.0 / row(cols[j][v], i)
            inv[v] = jnp.where(sub == i, r, inv[v])
            full = [jnp.where(sub == i, 0.0, cols[j][u]) if u == v else cols[j][u] for u in range(h)]
            m = [x * r for x in full]
            part = jnp.where(sub > i, m[v], 0.0)
            for k in range(j + 1, WIDE):
                s = row(cols[k][v], i)
                for u in range(h):
                    if k == j + 1:
                        cols[k][u] = cols[k][u] - (full[u] * s) * r
                    else:
                        cols[k][u] = cols[k][u] - m[u] * s
            ro, ra, rz = row(own[v], i), row(aug[v], i), row(zed[v], i)
            for u in range(h):
                if u >= v:
                    low = part if u == v else m[u]
                    own[u] = own[u] - low * ro
                    aug[u] = aug[u] - low * ra
                zed[u] = zed[u] - m[u] * rz
        rows, dones = [], []
        for u in range(h):
            root = jnp.sqrt(inv[u])
            at = base + 8 * u
            upper.append(jnp.where(lane >= at + sub, own[u] * root, 0.0))
            inverse.append(jnp.where(lane <= at + sub, aug[u] * root, 0.0))
            done = zed[u] * inv[u]
            dones.append(done)
            rows += [row(done, k) for k in range(8)]
        for t in near:
            s = [below[t][k] * rows[k] for k in range(WIDE)]
            while len(s) > 1:
                s = [s[k] + s[k + 1] for k in range(0, len(s), 2)]
            c[t] = jnp.where(inside, 0.0, c[t]) - s[0]
        far = range(p + 2 * h, n)
        if far:
            pad = [jnp.zeros((8, 128), F32)] * n
            for u in range(h):
                pad[p + u] = dones[u]
            change = jnp.dot(jnp.concatenate([c[t] for t in far], axis=0), jnp.concatenate(pad, axis=0),
                             preferred_element_type=F32, precision=lax.Precision.HIGHEST)
            for at, t in enumerate(far):
                c[t] = jnp.where(inside, 0.0, c[t]) - change[8 * at:8 * at + 8]
    return upper, inverse


def factor_kernel(total_ref, other_ref, out_ref, packed, work, inv):
    core = lax.rem(lax.axis_index("dp"), 2)
    packed[pl.ds(pl.multiple_of(core * HALF, HALF), HALF), :] = total_ref[...]
    packed[pl.ds(pl.multiple_of((1 - core) * HALF, HALF), HALF), :] = other_ref[...]
    unit = jnp.where(
        lax.broadcasted_iota(jnp.int32, (128, 128), 0) == lax.broadcasted_iota(jnp.int32, (128, 128), 1),
        1.0, 0.0).astype(BF16)
    row32 = lax.broadcasted_iota(jnp.int32, (32, 128), 0)
    lane128 = lax.broadcasted_iota(jnp.int32, (32, 128), 1)
    lane64 = lax.rem(lane128, 64)
    left = lane128 < 64
    outer = lane64 < 32
    for at in range(10):
        half, spot_in = divmod(at, 5)
        for u in range(2):
            base = HALF * half + 64 * spot_in + 32 * u
            raw = packed[base:base + 32, :]
            turned = nt_dot(unit, jnp.concatenate([raw] * 4, axis=0))
            wide = raw.astype(F32)
            spare = packed[HALF * half + 320:HALF * half + 336, :].astype(F32)[2 * spot_in + u:2 * spot_in + u + 1]
            own = jnp.where(left, turned[0:32], turned[64:96])
            cross = jnp.where(left, turned[32:64], turned[96:128])
            top = jnp.where(outer & (row32 > lane64), own, wide)
            low = jnp.where(row32 > lane64 - 32, pltpu.roll(wide, 32, 1), own)
            low = jnp.where(row32 == lane64 - 32, spare, low)
            low = jnp.where(outer, cross, low)
            work[128 * at + 64 * u:128 * at + 64 * u + 32, :] = top * (1.0 / 8192)
            work[128 * at + 64 * u + 32:128 * at + 64 * u + 64, :] = low * (1.0 / 8192)
    place = {ij: 128 * n for n, ij in enumerate(TILES)}
    sub = lax.broadcasted_iota(jnp.int32, (8, 128), 0)
    lane = lax.broadcasted_iota(jnp.int32, (8, 128), 1)
    for s in range(4):
        o = place[s, s]
        c = [work[o + 8 * t:o + 8 * t + 8, :] + jnp.where(lane == sub + 8 * t, DAMPING, 0.0) for t in range(16)]
        upper, inverse = factor_block(c)
        for t in range(16):
            out_ref[128 * s + 8 * t:128 * s + 8 * t + 8, 128 * s:128 * s + 128] = upper[t]
            inv[8 * t:8 * t + 8, :] = inverse[t]
        for j in range(s):
            out_ref[128 * s:128 * s + 128, 128 * j:128 * j + 128] = jnp.zeros((128, 128), F32)
        for j in range(s + 1, 4):
            a = work[place[s, j]:place[s, j] + 128, :]
            out_ref[128 * s:128 * s + 128, 128 * j:128 * j + 128] = jnp.dot(
                inv[...], a, preferred_element_type=F32, precision=lax.Precision.HIGHEST)
        for i in range(s + 1, 4):
            for j in range(i, 4):
                ri = out_ref[128 * s:128 * s + 128, 128 * i:128 * i + 128]
                rj = out_ref[128 * s:128 * s + 128, 128 * j:128 * j + 128]
                work[place[i, j]:place[i, j] + 128, :] -= lax.dot_general(
                    ri, rj, (((0,), (0,)), ((), ())), preferred_element_type=F32, precision=lax.Precision.HIGHEST)

def spot(y, x, core):
    return (y * 4 + x) * 2 + core


def moves(step):
    return [(spot(y, x, c), spot(*step(y, x, c)))
            for y in range(4) for x in range(4) for c in range(2)]


def shards(acts, grads, proj_in, block_vals, block_index, assign):
    ex, k_in = acts.shape
    k_out = grads.shape[1]
    hbm = pl.BlockSpec(memory_space=pltpu.HBM)
    vmem = pl.BlockSpec(memory_space=pltpu.VMEM)
    send = pl.pallas_call(
        project_kernel,
        out_shape=jax.ShapeDtypeStruct((8, 160, 128), BF16),
        in_specs=[hbm] * 6,
        out_specs=vmem,
        scratch_shapes=[
            pltpu.SMEM((block_index.shape[0],), jnp.int32),
            pltpu.VMEM((1, ex), jnp.int32),
            pltpu.VMEM((ex, k_in), BF16),
            pltpu.VMEM((ex, k_out), BF16),
            pltpu.VMEM((64, k_in), BF16),
            pltpu.VMEM((64, k_out), BF16),
            pltpu.SMEM((k_out // 128,), jnp.int32),
            pltpu.SemaphoreType.DMA((6,)),
            pltpu.SemaphoreType.DMA((k_out // 128,)),
        ],
        compiler_params=pltpu.CompilerParams(vmem_limit_bytes=16 << 20),
        name="project",
    )(*(pltpu.with_memory_space_constraint(x, pltpu.HBM) for x in (
        block_index, assign, acts, grads, proj_in.T, jnp.swapaxes(block_vals, 1, 2))))
    recv = lax.all_to_all(send, "mp", 0, 0, tiled=True)
    coords, keep, give = pl.pallas_call(
        gram_kernel,
        out_shape=(
            jax.ShapeDtypeStruct((160, 128), BF16),
            jax.ShapeDtypeStruct((HALF, 128), BF16),
            jax.ShapeDtypeStruct((HALF, 128), BF16),
        ),
        in_specs=[vmem],
        out_specs=(vmem, vmem, vmem),
        scratch_shapes=[pltpu.VMEM((FB, 256), BF16), pltpu.VMEM((2 * HALF, 128), BF16)],
        compiler_params=pltpu.CompilerParams(vmem_limit_bytes=12 << 20),
        name="gram",
    )(recv)
    features = pl.pallas_call(
        features_kernel,
        out_shape=jax.ShapeDtypeStruct((32, 4096), BF16),
        in_specs=[vmem],
        out_specs=vmem,
        cost_estimate=pl.CostEstimate(flops=2 * 32 * 64 * 4096, bytes_accessed=300000, transcendentals=0),
        compiler_params=pltpu.CompilerParams(vmem_limit_bytes=12 << 20),
        name="features",
    )(coords)
    total = keep + lax.ppermute(give, "dp", moves(lambda y, x, c: (y, x, 1 - c)))
    for ring in (lambda y, x, c, k: (y, (x + k) % 4, c), lambda y, x, c, k: ((y + k) % 4, x, c)):
        after, before, across = (
            lax.ppermute(total, "dp", moves(functools.partial(ring, k=k))).astype(F32) for k in (1, 3, 2))
        total = ((total.astype(F32) + across) + (after + before)).astype(BF16)
        total, features = lax.optimization_barrier((total, features))
    other = lax.ppermute(total, "dp", moves(lambda y, x, c: (y, x, 1 - c)))
    factor = pl.pallas_call(
        factor_kernel,
        out_shape=jax.ShapeDtypeStruct((FB, FB), F32),
        in_specs=[vmem, vmem],
        out_specs=vmem,
        scratch_shapes=[pltpu.VMEM((2 * HALF, 128), BF16), pltpu.VMEM((1280, 128), F32), pltpu.VMEM((128, 128), F32)],
        compiler_params=pltpu.CompilerParams(vmem_limit_bytes=12 << 20),
        name="factor",
    )(total, other).reshape(1, FB, FB)
    return features, factor


def solution(mesh):
    return jax.shard_map(
        shards,
        mesh=mesh,
        in_specs=(P("dp", "mp"), P("dp", "mp"), P(), P(), P(), P("dp", None)),
        out_specs=(P(("dp", "mp"), None), P("mp", None, None)),
        check_vma=False,
    )
```

```python
import functools

import jax
import jax.numpy as jnp
from jax import lax
from jax.experimental import pallas as pl
from jax.experimental.pallas import tpu as pltpu
from jax.sharding import PartitionSpec as P

FB = 512
DAMPING = 0.05
BF16 = jnp.bfloat16
F32 = jnp.float32
NT = (((1,), (1,)), ((), ()))


def nt_dot(a, b):
    return lax.dot_general(a, b, NT, preferred_element_type=F32)


def project_kernel(index_hbm, assign_hbm, acts_hbm, grads_hbm, proj_hbm, vals_hbm, send_ref,
                   index, assign, acts, grads, proj, vals, holder, sems, val_sems):
    me = lax.axis_index("mp")
    k_in = acts.shape[1]
    k_half = grads.shape[1] // 2
    blocks = val_sems.shape[0]
    in_copies = (
        pltpu.make_async_copy(index_hbm, index, sems.at[0]),
        pltpu.make_async_copy(proj_hbm.at[:, pl.ds(pl.multiple_of(me * k_in, 128), k_in)], proj, sems.at[1]),
        pltpu.make_async_copy(acts_hbm, acts, sems.at[2]),
        pltpu.make_async_copy(assign_hbm, assign, sems.at[3]),
    )
    out_copies = [
        pltpu.make_async_copy(grads_hbm.at[:, k_half * n:k_half * n + k_half],
                              grads.at[:, k_half * n:k_half * n + k_half], sems.at[4 + n])
        for n in range(2)
    ]
    for copy in (*in_copies, *out_copies):
        copy.start()
    vals[...] = jnp.zeros(vals.shape, BF16)
    first = me * blocks
    for j in range(blocks):
        holder[first + j] = -1
    in_copies[0].wait()

    def record(t, carry):
        holder[index[t]] = t
        return carry

    lax.fori_loop(0, index.shape[0], record, 0, unroll=32)

    def value_copy(j):
        return pltpu.make_async_copy(
            vals_hbm.at[holder[first + j]], vals.at[:, 128 * j:128 * j + 128], val_sems.at[j])

    for j in range(blocks):
        @pl.when(holder[first + j] >= 0)
        def _(j=j):
            value_copy(j).start()

    examples = acts.shape[0]
    in_copies[3].wait()
    rows = lax.broadcasted_iota(jnp.int32, (examples, examples), 0)
    order = jnp.where(rows == assign[...], 1.0, 0.0).astype(BF16)
    in_copies[1].wait()
    in_copies[2].wait()
    in_part = nt_dot(proj[...], acts[...]).astype(BF16)
    in_order = jnp.dot(in_part, order, preferred_element_type=F32)
    in_part = in_part.astype(F32)

    for j in range(blocks):
        @pl.when(holder[first + j] >= 0)
        def _(j=j):
            value_copy(j).wait()

    out_copies[0].wait()
    out_part = nt_dot(vals[:, 0:k_half], grads[:, 0:k_half])
    out_copies[1].wait()
    out_part = out_part + nt_dot(vals[:, k_half:2 * k_half], grads[:, k_half:2 * k_half])
    out_part = out_part.astype(BF16)
    for c in range(send_ref.shape[0]):
        send_ref[c, 0:64, :] = out_part[:, 0:128]
        send_ref[c, 64:128, :] = out_part[:, 128:256]
        tops = jnp.concatenate([in_part[8 * c:8 * c + 8, 0:128], in_part[8 * c:8 * c + 8, 128:256]], axis=0)
        send_ref[c, 128:144, :] = tops.astype(BF16)
        mine = jnp.concatenate(
            [in_order[16 * k:16 * k + 16, 32 * c:32 * c + 32] for k in range(4)], axis=1)
        send_ref[c, 144:160, :] = mine.astype(BF16)


TILES = [(i, j) for i in range(4) for j in range(i, 4)]
HALF = 336


def gram_kernel(recv_ref, coords_ref, keep_ref, give_ref, ft, packed):
    total = recv_ref[0].astype(F32)
    for c in range(1, recv_ref.shape[0]):
        total = total + recv_ref[c].astype(F32)
    coords = total.astype(BF16)
    coords_ref[...] = coords
    wide = coords.astype(F32)
    out_t = (wide[0:64], wide[64:128])
    in_t = (wide[128:136], wide[136:144])
    for p in range(8):
        for h in range(2):
            ft[64 * p:64 * p + 64, 128 * h:128 * h + 128] = (in_t[h][p:p + 1] * out_t[h]).astype(BF16)
    row32 = lax.broadcasted_iota(jnp.int32, (32, 128), 0)
    lane64 = lax.rem(lax.broadcasted_iota(jnp.int32, (32, 128), 1), 64)
    from_low = (lane64 < 32) & (row32 > lane64)
    on_diagonal = lane64 == row32 + 32
    left = lax.broadcasted_iota(jnp.int32, (32, 128), 1) < 64
    for half in range(2):
        spare = []
        for at, (i, j) in enumerate(TILES[5 * half:5 * half + 5]):
            tile = nt_dot(ft[128 * i:128 * i + 128, :], ft[128 * j:128 * j + 128, :])
            for u in range(2):
                top, low = tile[64 * u:64 * u + 32], tile[64 * u + 32:64 * u + 64]
                one = jnp.where(from_low, pltpu.roll(low, 96, 1), top)
                last = jnp.sum(jnp.where(on_diagonal, low, 0.0), axis=0, keepdims=True)
                if i == j and u == 0:
                    first = (one, last)
                elif i == j:
                    one = jnp.where(left, pltpu.roll(first[0], 64, 1), one)
                    last = jnp.where(left[0:1], pltpu.roll(first[1], 64, 1), last)
                packed[HALF * half + 64 * at + 32 * u:HALF * half + 64 * at + 32 * u + 32, :] = one.astype(BF16)
                spare.append(last)
        spare.append(jnp.zeros((6, 128), F32))
        packed[HALF * half + 320:HALF * half + 336, :] = jnp.concatenate(spare, axis=0).astype(BF16)
    core = lax.rem(lax.axis_index("dp"), 2)
    keep_ref[...] = packed[pl.ds(pl.multiple_of(core * HALF, HALF), HALF), :]
    give_ref[...] = packed[pl.ds(pl.multiple_of((1 - core) * HALF, HALF), HALF), :]


def features_kernel(assign_ref, coords_ref, features_ref):
    me = lax.axis_index("mp")
    coords = coords_ref[...]
    picked = jnp.concatenate([coords[0:64], coords[64:128]], axis=1)
    rows = lax.broadcasted_iota(jnp.int32, (32, 256), 0)
    cols = lax.broadcasted_iota(jnp.int32, (32, 256), 1)
    pick = jnp.where(cols == rows + 32 * me, 1.0, 0.0).astype(BF16)
    examples = lax.broadcasted_iota(jnp.int32, (256, 256), 0)
    order = jnp.where(examples == assign_ref[...], 1.0, 0.0).astype(BF16)
    outs = nt_dot(pick, jnp.dot(picked, order, preferred_element_type=F32).astype(BF16))
    wide = coords[144:160].astype(F32)
    mine = jnp.concatenate([wide[:, 32 * k:32 * k + 32] for k in range(4)], axis=0).astype(BF16)
    turn = jnp.where(
        lax.broadcasted_iota(jnp.int32, (32, 32), 0) == lax.broadcasted_iota(jnp.int32, (32, 32), 1),
        1.0, 0.0).astype(BF16)
    ins = nt_dot(turn, mine).astype(BF16)
    both = jnp.concatenate([outs, outs], axis=1)
    step = 512
    for at in range(features_ref.shape[1] // step):
        p = lax.broadcasted_iota(jnp.int32, (64, step), 0)
        f = lax.broadcasted_iota(jnp.int32, (64, step), 1)
        spread = jnp.where(p == (step // 64) * at + lax.div(f, 64), 1.0, 0.0).astype(BF16)
        left = jnp.dot(ins, spread, preferred_element_type=F32)
        for w in range(step // 128):
            features_ref[:, step * at + 128 * w:step * at + 128 * w + 128] = (
                left[:, 128 * w:128 * w + 128] * both).astype(BF16)


def spread_lane(x, at):
    return jnp.take_along_axis(x, jnp.full((8, 128), at, jnp.int32), axis=1)

def row(x, j):
    return jnp.broadcast_to(x[j:j + 1, :], (8, 128))

def split(x):
    high = x.astype(BF16)
    return high, (x - high.astype(F32)).astype(BF16)


def close_dot(a, b, dims):
    (ah, al), (bh, bl) = split(a), split(b)

    def one(x, y):
        return lax.dot_general(x, y, (dims, ((), ())), preferred_element_type=F32)

    return one(ah, bh) + (one(ah, bl) + one(al, bh))


NN = ((1,), (0,))
TN = ((0,), (0,))

WIDE = 16


def factor_block(c):
    sub = lax.broadcasted_iota(jnp.int32, (8, 128), 0)
    lane = lax.broadcasted_iota(jnp.int32, (8, 128), 1)
    n = len(c)
    h = WIDE // 8
    upper, inverse = [], []
    for p in range(0, n, h):
        base = 8 * p
        inside = (lane >= base) & (lane < base + WIDE)
        own = [c[p + u] for u in range(h)]
        cols = [[spread_lane(own[u], base + k) for u in range(h)] for k in range(WIDE)]
        if p:
            cols[0][0] = cols[0][0] + 0.0 * (cols[WIDE - 1][h - 1] + cols[WIDE - 2][h - 1])
        aug = [jnp.where(inside, jnp.where(lane - base == sub + 8 * u, 1.0, 0.0), own[u]) for u in range(h)]
        zed = list(aug)
        near = range(p + h, min(p + 2 * h, n))
        below = {t: [spread_lane(c[t], base + k) for k in range(WIDE)] for t in near}
        inv = [jnp.zeros((8, 128), F32) for _ in range(h)]
        for j in range(WIDE):
            v, i = divmod(j, 8)
            r = 1.0 / row(cols[j][v], i)
            inv[v] = jnp.where(sub == i, r, inv[v])
            full = [jnp.where(sub == i, 0.0, cols[j][u]) if u == v else cols[j][u] for u in range(h)]
            m = [x * r for x in full]
            part = jnp.where(sub > i, m[v], 0.0)
            for k in range(j + 1, WIDE):
                s = row(cols[k][v], i)
                for u in range(h):
                    if k == j + 1:
                        cols[k][u] = cols[k][u] - (full[u] * s) * r
                    else:
                        cols[k][u] = cols[k][u] - m[u] * s
            ro, ra, rz = row(own[v], i), row(aug[v], i), row(zed[v], i)
            for u in range(h):
                if u >= v:
                    low = part if u == v else m[u]
                    own[u] = own[u] - low * ro
                    aug[u] = aug[u] - low * ra
                zed[u] = zed[u] - m[u] * rz
        rows, dones = [], []
        for u in range(h):
            root = jnp.sqrt(inv[u])
            at = base + 8 * u
            upper.append(jnp.where(lane >= at + sub, own[u] * root, 0.0))
            inverse.append(jnp.where(lane <= at + sub, aug[u] * root, 0.0))
            done = zed[u] * inv[u]
            dones.append(done)
            rows += [row(done, k) for k in range(8)]
        for t in near:
            s = [below[t][k] * rows[k] for k in range(WIDE)]
            while len(s) > 1:
                s = [s[k] + s[k + 1] for k in range(0, len(s), 2)]
            c[t] = jnp.where(inside, 0.0, c[t]) - s[0]
        far = range(p + 2 * h, n)
        if far:
            pad = [jnp.zeros((8, 128), F32)] * n
            for u in range(h):
                pad[p + u] = dones[u]
            change = close_dot(jnp.concatenate([c[t] for t in far], axis=0), jnp.concatenate(pad, axis=0), NN)
            for at, t in enumerate(far):
                c[t] = jnp.where(inside, 0.0, c[t]) - change[8 * at:8 * at + 8]
    return upper, inverse


def factor_kernel(total_ref, other_ref, out_hbm, out, packed, work, inv, sems):
    core = lax.rem(lax.axis_index("dp"), 2)
    packed[pl.ds(pl.multiple_of(core * HALF, HALF), HALF), :] = total_ref[...]
    packed[pl.ds(pl.multiple_of((1 - core) * HALF, HALF), HALF), :] = other_ref[...]
    unit = jnp.where(
        lax.broadcasted_iota(jnp.int32, (128, 128), 0) == lax.broadcasted_iota(jnp.int32, (128, 128), 1),
        1.0, 0.0).astype(BF16)
    row32 = lax.broadcasted_iota(jnp.int32, (32, 128), 0)
    lane128 = lax.broadcasted_iota(jnp.int32, (32, 128), 1)
    lane64 = lax.rem(lane128, 64)
    left = lane128 < 64
    outer = lane64 < 32
    for at in range(10):
        half, spot_in = divmod(at, 5)
        for u in range(2):
            base = HALF * half + 64 * spot_in + 32 * u
            raw = packed[base:base + 32, :]
            turned = nt_dot(unit, jnp.concatenate([raw] * 4, axis=0))
            wide = raw.astype(F32)
            spare = packed[HALF * half + 320:HALF * half + 336, :].astype(F32)[2 * spot_in + u:2 * spot_in + u + 1]
            own = jnp.where(left, turned[0:32], turned[64:96])
            cross = jnp.where(left, turned[32:64], turned[96:128])
            top = jnp.where(outer & (row32 > lane64), own, wide)
            low = jnp.where(row32 > lane64 - 32, pltpu.roll(wide, 32, 1), own)
            low = jnp.where(row32 == lane64 - 32, spare, low)
            low = jnp.where(outer, cross, low)
            work[128 * at + 64 * u:128 * at + 64 * u + 32, :] = top * (1.0 / 8192)
            work[128 * at + 64 * u + 32:128 * at + 64 * u + 64, :] = low * (1.0 / 8192)
    place = {ij: 128 * n for n, ij in enumerate(TILES)}
    sub = lax.broadcasted_iota(jnp.int32, (8, 128), 0)
    lane = lax.broadcasted_iota(jnp.int32, (8, 128), 1)
    done = [pltpu.make_async_copy(out.at[128 * s:128 * s + 128, :], out_hbm.at[128 * s:128 * s + 128, :], sems.at[s]) for s in range(4)]
    for s in range(4):
        o = place[s, s]
        c = [work[o + 8 * t:o + 8 * t + 8, :] + jnp.where(lane == sub + 8 * t, DAMPING, 0.0) for t in range(16)]
        upper, inverse = factor_block(c)
        if s:
            done[s - 1].start()
        for t in range(16):
            out[128 * s + 8 * t:128 * s + 8 * t + 8, 128 * s:128 * s + 128] = upper[t]
            inv[8 * t:8 * t + 8, :] = inverse[t]
        for j in range(s):
            out[128 * s:128 * s + 128, 128 * j:128 * j + 128] = jnp.zeros((128, 128), F32)
        for j in range(s + 1, 4):
            a = work[place[s, j]:place[s, j] + 128, :]
            out[128 * s:128 * s + 128, 128 * j:128 * j + 128] = close_dot(inv[...], a, NN)
        for i in range(s + 1, 4):
            for j in range(i, 4):
                ri = out[128 * s:128 * s + 128, 128 * i:128 * i + 128]
                rj = out[128 * s:128 * s + 128, 128 * j:128 * j + 128]
                work[place[i, j]:place[i, j] + 128, :] -= close_dot(ri, rj, TN)
    done[3].start()
    for copy in done:
        copy.wait()


def spot(y, x, core):
    return (y * 4 + x) * 2 + core


def moves(step):
    return [(spot(y, x, c), spot(*step(y, x, c)))
            for y in range(4) for x in range(4) for c in range(2)]


def shards(acts, grads, proj_in, block_vals, block_index, assign):
    ex, k_in = acts.shape
    k_out = grads.shape[1]
    mp_count = lax.axis_size("mp")
    hbm = pl.BlockSpec(memory_space=pltpu.HBM)
    vmem = pl.BlockSpec(memory_space=pltpu.VMEM)
    send = pl.pallas_call(
        project_kernel,
        out_shape=jax.ShapeDtypeStruct((8, 160, 128), BF16),
        in_specs=[hbm] * 6,
        out_specs=vmem,
        scratch_shapes=[
            pltpu.SMEM((block_index.shape[0],), jnp.int32),
            pltpu.VMEM((1, ex), jnp.int32),
            pltpu.VMEM((ex, k_in), BF16),
            pltpu.VMEM((ex, k_out), BF16),
            pltpu.VMEM((64, k_in), BF16),
            pltpu.VMEM((64, k_out), BF16),
            pltpu.SMEM((mp_count * k_out // 128,), jnp.int32),
            pltpu.SemaphoreType.DMA((6,)),
            pltpu.SemaphoreType.DMA((k_out // 128,)),
        ],
        compiler_params=pltpu.CompilerParams(vmem_limit_bytes=16 << 20),
        name="project",
    )(*(pltpu.with_memory_space_constraint(x, pltpu.HBM) for x in (
        block_index, assign, acts, grads, proj_in.T, jnp.swapaxes(block_vals, 1, 2))))
    recv = lax.all_to_all(send, "mp", 0, 0, tiled=True)
    coords, keep, give = pl.pallas_call(
        gram_kernel,
        out_shape=(
            jax.ShapeDtypeStruct((160, 128), BF16),
            jax.ShapeDtypeStruct((HALF, 128), BF16),
            jax.ShapeDtypeStruct((HALF, 128), BF16),
        ),
        in_specs=[vmem],
        out_specs=(vmem, vmem, vmem),
        scratch_shapes=[pltpu.VMEM((FB, 256), BF16), pltpu.VMEM((2 * HALF, 128), BF16)],
        compiler_params=pltpu.CompilerParams(vmem_limit_bytes=12 << 20),
        name="gram",
    )(recv)
    features = pl.pallas_call(
        features_kernel,
        out_shape=jax.ShapeDtypeStruct((32, 4096), BF16),
        in_specs=[vmem, vmem],
        out_specs=vmem,
        cost_estimate=pl.CostEstimate(flops=2 * 32 * 64 * 4096, bytes_accessed=300000, transcendentals=0),
        compiler_params=pltpu.CompilerParams(vmem_limit_bytes=12 << 20),
        name="features",
    )(assign, coords)
    total = keep + lax.ppermute(give, "dp", moves(lambda y, x, c: (y, x, 1 - c)))
    for ring in (lambda y, x, c, k: (y, (x + k) % 4, c), lambda y, x, c, k: ((y + k) % 4, x, c)):
        after, before, across = (
            lax.ppermute(total, "dp", moves(functools.partial(ring, k=k))).astype(F32) for k in (1, 3, 2))
        total = ((total.astype(F32) + across) + (after + before)).astype(BF16)
        total, features = lax.optimization_barrier((total, features))
    other = lax.ppermute(total, "dp", moves(lambda y, x, c: (y, x, 1 - c)))
    factor = pl.pallas_call(
        factor_kernel,
        out_shape=jax.ShapeDtypeStruct((FB, FB), F32),
        in_specs=[vmem, vmem],
        out_specs=hbm,
        scratch_shapes=[
            pltpu.VMEM((FB, FB), F32),
            pltpu.VMEM((2 * HALF, 128), BF16),
            pltpu.VMEM((1280, 128), F32),
            pltpu.VMEM((128, 128), F32),
            pltpu.SemaphoreType.DMA((4,)),
        ],
        compiler_params=pltpu.CompilerParams(vmem_limit_bytes=12 << 20),
        name="factor",
    )(total, other).reshape(1, FB, FB)
    return features, factor


def solution(mesh):
    return jax.shard_map(
        shards,
        mesh=mesh,
        in_specs=(P("dp", "mp"), P("dp", "mp"), P(), P(), P(), P("dp", None)),
        out_specs=(P(("dp", "mp"), None), P("mp", None, None)),
        check_vma=False,
    )
```

```python
import functools

import jax
import jax.numpy as jnp
from jax import lax
from jax.experimental import pallas as pl
from jax.experimental.pallas import tpu as pltpu
from jax.sharding import PartitionSpec as P

FB = 512
DAMPING = 0.05
BF16 = jnp.bfloat16
F32 = jnp.float32
NT = (((1,), (1,)), ((), ()))


def nt_dot(a, b):
    return lax.dot_general(a, b, NT, preferred_element_type=F32)


def project_kernel(index_hbm, assign_hbm, acts_hbm, grads_hbm, proj_hbm, vals_hbm, send_ref,
                   index, assign, acts, grads, proj, vals, holder, sems, val_sems):
    me = lax.axis_index("mp")
    k_in = acts.shape[1]
    k_half = grads.shape[1] // 2
    blocks = val_sems.shape[0]
    in_copies = (
        pltpu.make_async_copy(index_hbm, index, sems.at[0]),
        pltpu.make_async_copy(proj_hbm.at[:, pl.ds(pl.multiple_of(me * k_in, 128), k_in)], proj, sems.at[1]),
        pltpu.make_async_copy(acts_hbm, acts, sems.at[2]),
        pltpu.make_async_copy(assign_hbm, assign, sems.at[3]),
    )
    out_copies = [
        pltpu.make_async_copy(grads_hbm.at[:, k_half * n:k_half * n + k_half],
                              grads.at[:, k_half * n:k_half * n + k_half], sems.at[4 + n])
        for n in range(2)
    ]
    for copy in (*in_copies, *out_copies):
        copy.start()
    vals[...] = jnp.zeros(vals.shape, BF16)
    first = me * blocks
    for j in range(blocks):
        holder[first + j] = -1
    in_copies[0].wait()

    def record(t, carry):
        holder[index[t]] = t
        return carry

    lax.fori_loop(0, index.shape[0], record, 0, unroll=32)

    def value_copy(j):
        return pltpu.make_async_copy(
            vals_hbm.at[holder[first + j]], vals.at[:, 128 * j:128 * j + 128], val_sems.at[j])

    for j in range(blocks):
        @pl.when(holder[first + j] >= 0)
        def _(j=j):
            value_copy(j).start()

    examples = acts.shape[0]
    in_copies[3].wait()
    rows = lax.broadcasted_iota(jnp.int32, (examples, examples), 0)
    order = jnp.where(rows == assign[...], 1.0, 0.0).astype(BF16)
    in_copies[1].wait()
    in_copies[2].wait()
    in_part = nt_dot(proj[...], acts[...]).astype(BF16)
    in_order = jnp.dot(in_part, order, preferred_element_type=F32)
    in_part = in_part.astype(F32)

    for j in range(blocks):
        @pl.when(holder[first + j] >= 0)
        def _(j=j):
            value_copy(j).wait()

    out_copies[0].wait()
    out_part = nt_dot(vals[:, 0:k_half], grads[:, 0:k_half])
    out_copies[1].wait()
    out_part = out_part + nt_dot(vals[:, k_half:2 * k_half], grads[:, k_half:2 * k_half])
    out_part = out_part.astype(BF16)
    for c in range(send_ref.shape[0]):
        send_ref[c, 0:64, :] = out_part[:, 0:128]
        send_ref[c, 64:128, :] = out_part[:, 128:256]
        tops = jnp.concatenate([in_part[8 * c:8 * c + 8, 0:128], in_part[8 * c:8 * c + 8, 128:256]], axis=0)
        send_ref[c, 128:144, :] = tops.astype(BF16)
        mine = jnp.concatenate(
            [in_order[16 * k:16 * k + 16, 32 * c:32 * c + 32] for k in range(4)], axis=1)
        send_ref[c, 144:160, :] = mine.astype(BF16)


TILES = [(i, j) for i in range(4) for j in range(i, 4)]
HALF = 304
SLOTS = 8


def gram_kernel(recv_ref, coords_ref, keep_ref, give_ref, ft, packed):
    total = recv_ref[0].astype(F32)
    for c in range(1, recv_ref.shape[0]):
        total = total + recv_ref[c].astype(F32)
    coords = total.astype(BF16)
    coords_ref[...] = coords
    wide = coords.astype(F32)
    out_t = (wide[0:64], wide[64:128])
    in_t = (wide[128:136], wide[136:144])
    for p in range(8):
        for h in range(2):
            ft[64 * p:64 * p + 64, 128 * h:128 * h + 128] = (in_t[h][p:p + 1] * out_t[h]).astype(BF16)
    row32 = lax.broadcasted_iota(jnp.int32, (32, 128), 0)
    lane64 = lax.rem(lax.broadcasted_iota(jnp.int32, (32, 128), 1), 64)
    from_low = (lane64 < 32) & (row32 > lane64)
    on_diagonal = lane64 == row32 + 32
    left = lax.broadcasted_iota(jnp.int32, (32, 128), 1) < 64
    for half in range(2):
        spare, single, slot = [], [], 0
        for i, j in TILES[5 * half:5 * half + 5]:
            tile = nt_dot(ft[128 * i:128 * i + 128, :], ft[128 * j:128 * j + 128, :])
            for u in range(2):
                top, low = tile[64 * u:64 * u + 32], tile[64 * u + 32:64 * u + 64]
                one = jnp.where(from_low, pltpu.roll(low, 96, 1), top)
                spare.append(jnp.sum(jnp.where(on_diagonal, low, 0.0), axis=0, keepdims=True))
                if i == j and u == 1:
                    single.append(one)
                    spare[-1] = jnp.where(left[0:1], pltpu.roll(spare[-2], 64, 1), spare[-1])
                else:
                    packed[HALF * half + 32 * slot:HALF * half + 32 * slot + 32, :] = one.astype(BF16)
                    slot += 1
        one = jnp.where(left, pltpu.roll(single[1], 64, 1), single[0])
        packed[HALF * half + 32 * SLOTS:HALF * half + 32 * SLOTS + 32, :] = one.astype(BF16)
        spare.append(jnp.zeros((6, 128), F32))
        packed[HALF * half + HALF - 16:HALF * half + HALF, :] = jnp.concatenate(spare, axis=0).astype(BF16)
    core = lax.rem(lax.axis_index("dp"), 2)
    keep_ref[...] = packed[pl.ds(pl.multiple_of(core * HALF, HALF), HALF), :]
    give_ref[...] = packed[pl.ds(pl.multiple_of((1 - core) * HALF, HALF), HALF), :]


def features_kernel(assign_ref, coords_ref, features_ref):
    me = lax.axis_index("mp")
    coords = coords_ref[...]
    picked = jnp.concatenate([coords[0:64], coords[64:128]], axis=1)
    rows = lax.broadcasted_iota(jnp.int32, (32, 256), 0)
    cols = lax.broadcasted_iota(jnp.int32, (32, 256), 1)
    pick = jnp.where(cols == rows + 32 * me, 1.0, 0.0).astype(BF16)
    examples = lax.broadcasted_iota(jnp.int32, (256, 256), 0)
    order = jnp.where(examples == assign_ref[...], 1.0, 0.0).astype(BF16)
    outs = nt_dot(pick, jnp.dot(picked, order, preferred_element_type=F32).astype(BF16))
    wide = coords[144:160].astype(F32)
    mine = jnp.concatenate([wide[:, 32 * k:32 * k + 32] for k in range(4)], axis=0).astype(BF16)
    turn = jnp.where(
        lax.broadcasted_iota(jnp.int32, (32, 32), 0) == lax.broadcasted_iota(jnp.int32, (32, 32), 1),
        1.0, 0.0).astype(BF16)
    ins = nt_dot(turn, mine).astype(BF16)
    both = jnp.concatenate([outs, outs], axis=1)
    step = 512
    for at in range(features_ref.shape[1] // step):
        p = lax.broadcasted_iota(jnp.int32, (64, step), 0)
        f = lax.broadcasted_iota(jnp.int32, (64, step), 1)
        spread = jnp.where(p == (step // 64) * at + lax.div(f, 64), 1.0, 0.0).astype(BF16)
        left = jnp.dot(ins, spread, preferred_element_type=F32)
        for w in range(step // 128):
            features_ref[:, step * at + 128 * w:step * at + 128 * w + 128] = (
                left[:, 128 * w:128 * w + 128] * both).astype(BF16)


def spread_lane(x, at):
    return jnp.take_along_axis(x, jnp.full((8, 128), at, jnp.int32), axis=1)

def row(x, j):
    return jnp.broadcast_to(x[j:j + 1, :], (8, 128))

def split(x):
    high = x.astype(BF16)
    return high, (x - high.astype(F32)).astype(BF16)


def close_dot(a, b, dims):
    (ah, al), (bh, bl) = split(a), split(b)

    def one(x, y):
        return lax.dot_general(x, y, (dims, ((), ())), preferred_element_type=F32)

    return one(ah, bh) + (one(ah, bl) + one(al, bh))


NN = ((1,), (0,))
TN = ((0,), (0,))

WIDE = 16


def factor_block(c):
    sub = lax.broadcasted_iota(jnp.int32, (8, 128), 0)
    lane = lax.broadcasted_iota(jnp.int32, (8, 128), 1)
    n = len(c)
    h = WIDE // 8
    upper, inverse = [], []
    for p in range(0, n, h):
        base = 8 * p
        inside = (lane >= base) & (lane < base + WIDE)
        own = [c[p + u] for u in range(h)]
        cols = [[spread_lane(own[u], base + k) for u in range(h)] for k in range(WIDE)]
        if p:
            cols[0][0] = cols[0][0] + 0.0 * (cols[WIDE - 1][h - 1] + cols[WIDE - 2][h - 1])
        aug = [jnp.where(inside, jnp.where(lane - base == sub + 8 * u, 1.0, 0.0), own[u]) for u in range(h)]
        zed = list(aug)
        near = range(p + h, min(p + 2 * h, n))
        below = {t: [spread_lane(c[t], base + k) for k in range(WIDE)] for t in near}
        inv = [jnp.zeros((8, 128), F32) for _ in range(h)]
        for j in range(WIDE):
            v, i = divmod(j, 8)
            r = 1.0 / row(cols[j][v], i)
            inv[v] = jnp.where(sub == i, r, inv[v])
            full = [jnp.where(sub == i, 0.0, cols[j][u]) if u == v else cols[j][u] for u in range(h)]
            m = [x * r for x in full]
            part = jnp.where(sub > i, m[v], 0.0)
            for k in range(j + 1, WIDE):
                s = row(cols[k][v], i)
                for u in range(h):
                    if k == j + 1:
                        cols[k][u] = cols[k][u] - (full[u] * s) * r
                    else:
                        cols[k][u] = cols[k][u] - m[u] * s
            ro, ra, rz = row(own[v], i), row(aug[v], i), row(zed[v], i)
            for u in range(h):
                if u >= v:
                    low = part if u == v else m[u]
                    own[u] = own[u] - low * ro
                    aug[u] = aug[u] - low * ra
                zed[u] = zed[u] - m[u] * rz
        rows, dones = [], []
        for u in range(h):
            root = jnp.sqrt(inv[u])
            at = base + 8 * u
            upper.append(jnp.where(lane >= at + sub, own[u] * root, 0.0))
            inverse.append(jnp.where(lane <= at + sub, aug[u] * root, 0.0))
            done = zed[u] * inv[u]
            dones.append(done)
            rows += [row(done, k) for k in range(8)]
        for t in near:
            s = [below[t][k] * rows[k] for k in range(WIDE)]
            while len(s) > 1:
                s = [s[k] + s[k + 1] for k in range(0, len(s), 2)]
            c[t] = jnp.where(inside, 0.0, c[t]) - s[0]
        far = range(p + 2 * h, n)
        if far:
            pad = [jnp.zeros((8, 128), F32)] * n
            for u in range(h):
                pad[p + u] = dones[u]
            change = close_dot(jnp.concatenate([c[t] for t in far], axis=0), jnp.concatenate(pad, axis=0), NN)
            for at, t in enumerate(far):
                c[t] = jnp.where(inside, 0.0, c[t]) - change[8 * at:8 * at + 8]
    return upper, inverse


def factor_kernel(total_ref, other_ref, out_hbm, out, packed, work, inv, sems):
    core = lax.rem(lax.axis_index("dp"), 2)
    packed[pl.ds(pl.multiple_of(core * HALF, HALF), HALF), :] = total_ref[...]
    packed[pl.ds(pl.multiple_of((1 - core) * HALF, HALF), HALF), :] = other_ref[...]
    unit = jnp.where(
        lax.broadcasted_iota(jnp.int32, (128, 128), 0) == lax.broadcasted_iota(jnp.int32, (128, 128), 1),
        1.0, 0.0).astype(BF16)
    row32 = lax.broadcasted_iota(jnp.int32, (32, 128), 0)
    lane128 = lax.broadcasted_iota(jnp.int32, (32, 128), 1)
    lane64 = lax.rem(lane128, 64)
    left = lane128 < 64
    outer = lane64 < 32
    slots = [0, 0]
    for at, (i, j) in enumerate(TILES):
        half, spot_in = divmod(at, 5)
        for u in range(2):
            if i == j and u == 1:
                first = wide
                single = packed[HALF * half + 32 * SLOTS:HALF * half + 32 * SLOTS + 32, :].astype(F32)
                if i % 2:
                    single = pltpu.roll(single, 64, 1)
                wide = jnp.where(left, pltpu.roll(first, 64, 1), single)
                raw = wide.astype(BF16)
            else:
                base = HALF * half + 32 * slots[half]
                slots[half] += 1
                raw = packed[base:base + 32, :]
                wide = raw.astype(F32)
            turned = nt_dot(unit, jnp.concatenate([raw] * 4, axis=0))
            spare = packed[HALF * half + HALF - 16:HALF * half + HALF, :].astype(F32)[2 * spot_in + u:2 * spot_in + u + 1]
            own = jnp.where(left, turned[0:32], turned[64:96])
            cross = jnp.where(left, turned[32:64], turned[96:128])
            top = jnp.where(outer & (row32 > lane64), own, wide)
            low = jnp.where(row32 > lane64 - 32, pltpu.roll(wide, 32, 1), own)
            low = jnp.where(row32 == lane64 - 32, spare, low)
            low = jnp.where(outer, cross, low)
            work[128 * at + 64 * u:128 * at + 64 * u + 32, :] = top * (1.0 / 8192)
            work[128 * at + 64 * u + 32:128 * at + 64 * u + 64, :] = low * (1.0 / 8192)
    place = {ij: 128 * n for n, ij in enumerate(TILES)}
    sub = lax.broadcasted_iota(jnp.int32, (8, 128), 0)
    lane = lax.broadcasted_iota(jnp.int32, (8, 128), 1)
    done = [pltpu.make_async_copy(out.at[128 * s:128 * s + 128, :], out_hbm.at[128 * s:128 * s + 128, :], sems.at[s]) for s in range(4)]
    for s in range(4):
        o = place[s, s]
        c = [work[o + 8 * t:o + 8 * t + 8, :] + jnp.where(lane == sub + 8 * t, DAMPING, 0.0) for t in range(16)]
        upper, inverse = factor_block(c)
        if s:
            done[s - 1].start()
        for t in range(16):
            out[128 * s + 8 * t:128 * s + 8 * t + 8, 128 * s:128 * s + 128] = upper[t]
            inv[8 * t:8 * t + 8, :] = inverse[t]
        for j in range(s):
            out[128 * s:128 * s + 128, 128 * j:128 * j + 128] = jnp.zeros((128, 128), F32)
        for j in range(s + 1, 4):
            a = work[place[s, j]:place[s, j] + 128, :]
            out[128 * s:128 * s + 128, 128 * j:128 * j + 128] = close_dot(inv[...], a, NN)
        for i in range(s + 1, 4):
            for j in range(i, 4):
                ri = out[128 * s:128 * s + 128, 128 * i:128 * i + 128]
                rj = out[128 * s:128 * s + 128, 128 * j:128 * j + 128]
                work[place[i, j]:place[i, j] + 128, :] -= close_dot(ri, rj, TN)
    done[3].start()
    for copy in done:
        copy.wait()


def spot(y, x, core):
    return (y * 4 + x) * 2 + core


def moves(step):
    return [(spot(y, x, c), spot(*step(y, x, c)))
            for y in range(4) for x in range(4) for c in range(2)]


def shards(acts, grads, proj_in, block_vals, block_index, assign):
    ex, k_in = acts.shape
    k_out = grads.shape[1]
    mp_count = lax.axis_size("mp")
    hbm = pl.BlockSpec(memory_space=pltpu.HBM)
    vmem = pl.BlockSpec(memory_space=pltpu.VMEM)
    send = pl.pallas_call(
        project_kernel,
        out_shape=jax.ShapeDtypeStruct((8, 160, 128), BF16),
        in_specs=[hbm] * 6,
        out_specs=vmem,
        scratch_shapes=[
            pltpu.SMEM((block_index.shape[0],), jnp.int32),
            pltpu.VMEM((1, ex), jnp.int32),
            pltpu.VMEM((ex, k_in), BF16),
            pltpu.VMEM((ex, k_out), BF16),
            pltpu.VMEM((64, k_in), BF16),
            pltpu.VMEM((64, k_out), BF16),
            pltpu.SMEM((mp_count * k_out // 128,), jnp.int32),
            pltpu.SemaphoreType.DMA((6,)),
            pltpu.SemaphoreType.DMA((k_out // 128,)),
        ],
        compiler_params=pltpu.CompilerParams(vmem_limit_bytes=16 << 20),
        name="project",
    )(*(pltpu.with_memory_space_constraint(x, pltpu.HBM) for x in (
        block_index, assign, acts, grads, proj_in.T, jnp.swapaxes(block_vals, 1, 2))))
    recv = lax.all_to_all(send, "mp", 0, 0, tiled=True)
    coords, keep, give = pl.pallas_call(
        gram_kernel,
        out_shape=(
            jax.ShapeDtypeStruct((160, 128), BF16),
            jax.ShapeDtypeStruct((HALF, 128), BF16),
            jax.ShapeDtypeStruct((HALF, 128), BF16),
        ),
        in_specs=[vmem],
        out_specs=(vmem, vmem, vmem),
        scratch_shapes=[pltpu.VMEM((FB, 256), BF16), pltpu.VMEM((2 * HALF, 128), BF16)],
        compiler_params=pltpu.CompilerParams(vmem_limit_bytes=12 << 20),
        name="gram",
    )(recv)
    features = pl.pallas_call(
        features_kernel,
        out_shape=jax.ShapeDtypeStruct((32, 4096), BF16),
        in_specs=[vmem, vmem],
        out_specs=vmem,
        cost_estimate=pl.CostEstimate(flops=2 * 32 * 64 * 4096, bytes_accessed=300000, transcendentals=0),
        compiler_params=pltpu.CompilerParams(vmem_limit_bytes=12 << 20),
        name="features",
    )(assign, coords)
    total = keep + lax.ppermute(give, "dp", moves(lambda y, x, c: (y, x, 1 - c)))
    for ring in (lambda y, x, c, k: (y, (x + k) % 4, c), lambda y, x, c, k: ((y + k) % 4, x, c)):
        after, before, across = (
            lax.ppermute(total, "dp", moves(functools.partial(ring, k=k))).astype(F32) for k in (1, 3, 2))
        total = ((total.astype(F32) + across) + (after + before)).astype(BF16)
        total, features = lax.optimization_barrier((total, features))
    other = lax.ppermute(total, "dp", moves(lambda y, x, c: (y, x, 1 - c)))
    factor = pl.pallas_call(
        factor_kernel,
        out_shape=jax.ShapeDtypeStruct((FB, FB), F32),
        in_specs=[vmem, vmem],
        out_specs=hbm,
        scratch_shapes=[
            pltpu.VMEM((FB, FB), F32),
            pltpu.VMEM((2 * HALF, 128), BF16),
            pltpu.VMEM((1280, 128), F32),
            pltpu.VMEM((128, 128), F32),
            pltpu.SemaphoreType.DMA((4,)),
        ],
        compiler_params=pltpu.CompilerParams(vmem_limit_bytes=12 << 20),
        name="factor",
    )(total, other).reshape(1, FB, FB)
    return features, factor


def solution(mesh):
    return jax.shard_map(
        shards,
        mesh=mesh,
        in_specs=(P("dp", "mp"), P("dp", "mp"), P(), P(), P(), P("dp", None)),
        out_specs=(P(("dp", "mp"), None), P("mp", None, None)),
        check_vma=False,
    )
```

```python
import functools

import jax
import jax.numpy as jnp
from jax import lax
from jax.experimental import pallas as pl
from jax.experimental.pallas import tpu as pltpu
from jax.sharding import PartitionSpec as P

FB = 512
DAMPING = 0.05
BF16 = jnp.bfloat16
F32 = jnp.float32
NT = (((1,), (1,)), ((), ()))


def nt_dot(a, b):
    return lax.dot_general(a, b, NT, preferred_element_type=F32)


def project_kernel(index_hbm, assign_hbm, acts_hbm, grads_hbm, proj_hbm, vals_hbm, send_ref,
                   index, assign, acts, grads, proj, vals, holder, sems, val_sems):
    me = lax.axis_index("mp")
    k_in = acts.shape[1]
    cuts = (0, 2560, grads.shape[1])
    blocks = val_sems.shape[0]
    in_copies = (
        pltpu.make_async_copy(index_hbm, index, sems.at[0]),
        pltpu.make_async_copy(proj_hbm.at[:, pl.ds(pl.multiple_of(me * k_in, 128), k_in)], proj, sems.at[1]),
        pltpu.make_async_copy(acts_hbm, acts, sems.at[2]),
        pltpu.make_async_copy(assign_hbm, assign, sems.at[3]),
    )
    out_copies = [
        pltpu.make_async_copy(grads_hbm.at[:, cuts[n]:cuts[n + 1]], grads.at[:, cuts[n]:cuts[n + 1]], sems.at[4 + n])
        for n in range(2)
    ]
    for copy in (*in_copies, *out_copies):
        copy.start()
    vals[...] = jnp.zeros(vals.shape, BF16)
    first = me * blocks
    for j in range(blocks):
        holder[first + j] = -1
    in_copies[0].wait()

    def record(t, carry):
        holder[index[t]] = t
        return carry

    lax.fori_loop(0, index.shape[0], record, 0, unroll=32)

    def value_copy(j):
        return pltpu.make_async_copy(
            vals_hbm.at[holder[first + j]], vals.at[:, 128 * j:128 * j + 128], val_sems.at[j])

    for j in range(blocks):
        @pl.when(holder[first + j] >= 0)
        def _(j=j):
            value_copy(j).start()

    examples = acts.shape[0]
    in_copies[3].wait()
    rows = lax.broadcasted_iota(jnp.int32, (examples, examples), 0)
    order = jnp.where(rows == assign[...], 1.0, 0.0).astype(BF16)
    in_copies[1].wait()
    in_copies[2].wait()
    in_part = nt_dot(proj[...], acts[...]).astype(BF16)
    in_order = jnp.dot(in_part, order, preferred_element_type=F32)
    in_part = in_part.astype(F32)

    for j in range(blocks):
        @pl.when(holder[first + j] >= 0)
        def _(j=j):
            value_copy(j).wait()

    out_copies[0].wait()
    out_part = nt_dot(vals[:, 0:cuts[1]], grads[:, 0:cuts[1]])
    out_copies[1].wait()
    out_part = out_part + nt_dot(vals[:, cuts[1]:], grads[:, cuts[1]:])
    out_part = out_part.astype(BF16)
    for c in range(send_ref.shape[0]):
        send_ref[c, 0:64, :] = out_part[:, 0:128]
        send_ref[c, 64:128, :] = out_part[:, 128:256]
        tops = jnp.concatenate([in_part[8 * c:8 * c + 8, 0:128], in_part[8 * c:8 * c + 8, 128:256]], axis=0)
        send_ref[c, 128:144, :] = tops.astype(BF16)
        mine = jnp.concatenate(
            [in_order[16 * k:16 * k + 16, 32 * c:32 * c + 32] for k in range(4)], axis=1)
        send_ref[c, 144:160, :] = mine.astype(BF16)


TILES = [(i, j) for i in range(4) for j in range(i, 4)]
HALF = 304
SLOTS = 8


def gram_kernel(recv_ref, coords_ref, keep_ref, give_ref, ft, packed):
    total = recv_ref[0].astype(F32)
    for c in range(1, recv_ref.shape[0]):
        total = total + recv_ref[c].astype(F32)
    coords = total.astype(BF16)
    coords_ref[...] = coords
    wide = coords.astype(F32)
    out_t = (wide[0:64], wide[64:128])
    in_t = (wide[128:136], wide[136:144])
    for p in range(8):
        for h in range(2):
            ft[64 * p:64 * p + 64, 128 * h:128 * h + 128] = (in_t[h][p:p + 1] * out_t[h]).astype(BF16)
    row32 = lax.broadcasted_iota(jnp.int32, (32, 128), 0)
    lane64 = lax.rem(lax.broadcasted_iota(jnp.int32, (32, 128), 1), 64)
    from_low = (lane64 < 32) & (row32 > lane64)
    on_diagonal = lane64 == row32 + 32
    left = lax.broadcasted_iota(jnp.int32, (32, 128), 1) < 64
    for half in range(2):
        spare, single, slot = [], [], 0
        for i, j in TILES[5 * half:5 * half + 5]:
            tile = nt_dot(ft[128 * i:128 * i + 128, :], ft[128 * j:128 * j + 128, :])
            for u in range(2):
                top, low = tile[64 * u:64 * u + 32], tile[64 * u + 32:64 * u + 64]
                one = jnp.where(from_low, pltpu.roll(low, 96, 1), top)
                spare.append(jnp.sum(jnp.where(on_diagonal, low, 0.0), axis=0, keepdims=True))
                if i == j and u == 1:
                    single.append(one)
                    spare[-1] = jnp.where(left[0:1], pltpu.roll(spare[-2], 64, 1), spare[-1])
                else:
                    packed[HALF * half + 32 * slot:HALF * half + 32 * slot + 32, :] = one.astype(BF16)
                    slot += 1
        one = jnp.where(left, pltpu.roll(single[1], 64, 1), single[0])
        packed[HALF * half + 32 * SLOTS:HALF * half + 32 * SLOTS + 32, :] = one.astype(BF16)
        spare.append(jnp.zeros((6, 128), F32))
        packed[HALF * half + HALF - 16:HALF * half + HALF, :] = jnp.concatenate(spare, axis=0).astype(BF16)
    core = lax.rem(lax.axis_index("dp"), 2)
    keep_ref[...] = packed[pl.ds(pl.multiple_of(core * HALF, HALF), HALF), :]
    give_ref[...] = packed[pl.ds(pl.multiple_of((1 - core) * HALF, HALF), HALF), :]


def features_kernel(assign_ref, coords_ref, features_ref):
    me = lax.axis_index("mp")
    coords = coords_ref[...]
    picked = jnp.concatenate([coords[0:64], coords[64:128]], axis=1)
    rows = lax.broadcasted_iota(jnp.int32, (32, 256), 0)
    cols = lax.broadcasted_iota(jnp.int32, (32, 256), 1)
    pick = jnp.where(cols == rows + 32 * me, 1.0, 0.0).astype(BF16)
    examples = lax.broadcasted_iota(jnp.int32, (256, 256), 0)
    order = jnp.where(examples == assign_ref[...], 1.0, 0.0).astype(BF16)
    outs = nt_dot(pick, jnp.dot(picked, order, preferred_element_type=F32).astype(BF16))
    wide = coords[144:160].astype(F32)
    mine = jnp.concatenate([wide[:, 32 * k:32 * k + 32] for k in range(4)], axis=0).astype(BF16)
    turn = jnp.where(
        lax.broadcasted_iota(jnp.int32, (32, 32), 0) == lax.broadcasted_iota(jnp.int32, (32, 32), 1),
        1.0, 0.0).astype(BF16)
    ins = nt_dot(turn, mine).astype(BF16)
    both = jnp.concatenate([outs, outs], axis=1)
    step = 512
    for at in range(features_ref.shape[1] // step):
        p = lax.broadcasted_iota(jnp.int32, (64, step), 0)
        f = lax.broadcasted_iota(jnp.int32, (64, step), 1)
        spread = jnp.where(p == (step // 64) * at + lax.div(f, 64), 1.0, 0.0).astype(BF16)
        left = jnp.dot(ins, spread, preferred_element_type=F32)
        for w in range(step // 128):
            features_ref[:, step * at + 128 * w:step * at + 128 * w + 128] = (
                left[:, 128 * w:128 * w + 128] * both).astype(BF16)


def spread_lane(x, at):
    return jnp.take_along_axis(x, jnp.full((8, 128), at, jnp.int32), axis=1)

def row(x, j):
    return jnp.broadcast_to(x[j:j + 1, :], (8, 128))

def split(x):
    high = x.astype(BF16)
    return high, (x - high.astype(F32)).astype(BF16)


def close_dot(a, b, dims):
    (ah, al), (bh, bl) = split(a), split(b)

    def one(x, y):
        return lax.dot_general(x, y, (dims, ((), ())), preferred_element_type=F32)

    return one(ah, bh) + (one(ah, bl) + one(al, bh))


NN = ((1,), (0,))
TN = ((0,), (0,))

WIDE = 16


def factor_block(c, invert):
    sub = lax.broadcasted_iota(jnp.int32, (8, 128), 0)
    lane = lax.broadcasted_iota(jnp.int32, (8, 128), 1)
    n = len(c)
    h = WIDE // 8
    upper, inverse = [], []
    for p in range(0, n, h):
        base = 8 * p
        inside = (lane >= base) & (lane < base + WIDE)
        own = [c[p + u] for u in range(h)]
        cols = [[spread_lane(own[u], base + k) for u in range(h)] for k in range(WIDE)]
        if p:
            cols[0][0] = cols[0][0] + 0.0 * (cols[WIDE - 1][h - 1] + cols[WIDE - 2][h - 1])
        aug = [jnp.where(inside, jnp.where(lane - base == sub + 8 * u, 1.0, 0.0), own[u]) for u in range(h)]
        if not invert:
            aug = list(own)
        zed = list(aug)
        near = range(p + h, min(p + 2 * h, n))
        below = {t: [spread_lane(c[t], base + k) for k in range(WIDE)] for t in near}
        inv = [jnp.zeros((8, 128), F32) for _ in range(h)]
        for j in range(WIDE):
            v, i = divmod(j, 8)
            r = 1.0 / row(cols[j][v], i)
            inv[v] = jnp.where(sub == i, r, inv[v])
            full = [jnp.where(sub == i, 0.0, cols[j][u]) if u == v else cols[j][u] for u in range(h)]
            m = [x * r for x in full]
            part = jnp.where(sub > i, m[v], 0.0)
            for k in range(j + 1, WIDE):
                s = row(cols[k][v], i)
                for u in range(h):
                    if k == j + 1:
                        cols[k][u] = cols[k][u] - (full[u] * s) * r
                    else:
                        cols[k][u] = cols[k][u] - m[u] * s
            ro, ra, rz = row(own[v], i), row(aug[v], i), row(zed[v], i)
            for u in range(h):
                if u >= v:
                    low = part if u == v else m[u]
                    own[u] = own[u] - low * ro
                    if invert:
                        aug[u] = aug[u] - low * ra
                zed[u] = zed[u] - m[u] * rz
        rows, dones = [], []
        for u in range(h):
            root = jnp.sqrt(inv[u])
            at = base + 8 * u
            upper.append(jnp.where(lane >= at + sub, own[u] * root, 0.0))
            inverse.append(jnp.where(lane <= at + sub, aug[u] * root, 0.0))
            done = zed[u] * inv[u]
            dones.append(done)
            rows += [row(done, k) for k in range(8)]
        for t in near:
            s = [below[t][k] * rows[k] for k in range(WIDE)]
            while len(s) > 1:
                s = [s[k] + s[k + 1] for k in range(0, len(s), 2)]
            c[t] = jnp.where(inside, 0.0, c[t]) - s[0]
        far = range(p + 2 * h, n)
        if far:
            pad = [jnp.zeros((8, 128), F32)] * n
            for u in range(h):
                pad[p + u] = dones[u]
            change = close_dot(jnp.concatenate([c[t] for t in far], axis=0), jnp.concatenate(pad, axis=0), NN)
            for at, t in enumerate(far):
                c[t] = jnp.where(inside, 0.0, c[t]) - change[8 * at:8 * at + 8]
    return upper, inverse


def factor_kernel(total_ref, other_ref, out_hbm, out, packed, work, inv, sems):
    core = lax.rem(lax.axis_index("dp"), 2)
    packed[pl.ds(pl.multiple_of(core * HALF, HALF), HALF), :] = total_ref[...]
    packed[pl.ds(pl.multiple_of((1 - core) * HALF, HALF), HALF), :] = other_ref[...]
    unit = jnp.where(
        lax.broadcasted_iota(jnp.int32, (128, 128), 0) == lax.broadcasted_iota(jnp.int32, (128, 128), 1),
        1.0, 0.0).astype(BF16)
    row32 = lax.broadcasted_iota(jnp.int32, (32, 128), 0)
    lane128 = lax.broadcasted_iota(jnp.int32, (32, 128), 1)
    lane64 = lax.rem(lane128, 64)
    left = lane128 < 64
    outer = lane64 < 32
    slots = [0, 0]
    for at, (i, j) in enumerate(TILES):
        half, spot_in = divmod(at, 5)
        for u in range(2):
            if i == j and u == 1:
                first = wide
                single = packed[HALF * half + 32 * SLOTS:HALF * half + 32 * SLOTS + 32, :].astype(F32)
                if i % 2:
                    single = pltpu.roll(single, 64, 1)
                wide = jnp.where(left, pltpu.roll(first, 64, 1), single)
                raw = wide.astype(BF16)
            else:
                base = HALF * half + 32 * slots[half]
                slots[half] += 1
                raw = packed[base:base + 32, :]
                wide = raw.astype(F32)
            turned = nt_dot(unit, jnp.concatenate([raw] * 4, axis=0))
            spare = packed[HALF * half + HALF - 16:HALF * half + HALF, :].astype(F32)[2 * spot_in + u:2 * spot_in + u + 1]
            own = jnp.where(left, turned[0:32], turned[64:96])
            cross = jnp.where(left, turned[32:64], turned[96:128])
            top = jnp.where(outer & (row32 > lane64), own, wide)
            low = jnp.where(row32 > lane64 - 32, pltpu.roll(wide, 32, 1), own)
            low = jnp.where(row32 == lane64 - 32, spare, low)
            low = jnp.where(outer, cross, low)
            work[128 * at + 64 * u:128 * at + 64 * u + 32, :] = top * (1.0 / 8192)
            work[128 * at + 64 * u + 32:128 * at + 64 * u + 64, :] = low * (1.0 / 8192)
    place = {ij: 128 * n for n, ij in enumerate(TILES)}
    sub = lax.broadcasted_iota(jnp.int32, (8, 128), 0)
    lane = lax.broadcasted_iota(jnp.int32, (8, 128), 1)
    done = [pltpu.make_async_copy(out.at[128 * s:128 * s + 128, :], out_hbm.at[128 * s:128 * s + 128, :], sems.at[s]) for s in range(4)]
    for s in range(4):
        o = place[s, s]
        c = [work[o + 8 * t:o + 8 * t + 8, :] + jnp.where(lane == sub + 8 * t, DAMPING, 0.0) for t in range(16)]
        upper, inverse = factor_block(c, s < 3)
        if s:
            done[s - 1].start()
        for t in range(16):
            out[128 * s + 8 * t:128 * s + 8 * t + 8, 128 * s:128 * s + 128] = upper[t]
            if s < 3:
                inv[8 * t:8 * t + 8, :] = inverse[t]
        for j in range(s):
            out[128 * s:128 * s + 128, 128 * j:128 * j + 128] = jnp.zeros((128, 128), F32)
        for j in range(s + 1, 4):
            a = work[place[s, j]:place[s, j] + 128, :]
            out[128 * s:128 * s + 128, 128 * j:128 * j + 128] = close_dot(inv[...], a, NN)
        for i in range(s + 1, 4):
            for j in range(i, 4):
                ri = out[128 * s:128 * s + 128, 128 * i:128 * i + 128]
                rj = out[128 * s:128 * s + 128, 128 * j:128 * j + 128]
                work[place[i, j]:place[i, j] + 128, :] -= close_dot(ri, rj, TN)
    done[3].start()
    for copy in done:
        copy.wait()


def spot(y, x, core):
    return (y * 4 + x) * 2 + core


def moves(step):
    return [(spot(y, x, c), spot(*step(y, x, c)))
            for y in range(4) for x in range(4) for c in range(2)]


def shards(acts, grads, proj_in, block_vals, block_index, assign):
    ex, k_in = acts.shape
    k_out = grads.shape[1]
    mp_count = lax.axis_size("mp")
    hbm = pl.BlockSpec(memory_space=pltpu.HBM)
    vmem = pl.BlockSpec(memory_space=pltpu.VMEM)
    send = pl.pallas_call(
        project_kernel,
        out_shape=jax.ShapeDtypeStruct((8, 160, 128), BF16),
        in_specs=[hbm] * 6,
        out_specs=vmem,
        scratch_shapes=[
            pltpu.SMEM((block_index.shape[0],), jnp.int32),
            pltpu.VMEM((1, ex), jnp.int32),
            pltpu.VMEM((ex, k_in), BF16),
            pltpu.VMEM((ex, k_out), BF16),
            pltpu.VMEM((64, k_in), BF16),
            pltpu.VMEM((64, k_out), BF16),
            pltpu.SMEM((mp_count * k_out // 128,), jnp.int32),
            pltpu.SemaphoreType.DMA((6,)),
            pltpu.SemaphoreType.DMA((k_out // 128,)),
        ],
        compiler_params=pltpu.CompilerParams(vmem_limit_bytes=16 << 20),
        name="project",
    )(*(pltpu.with_memory_space_constraint(x, pltpu.HBM) for x in (
        block_index, assign, acts, grads, proj_in.T, jnp.swapaxes(block_vals, 1, 2))))
    recv = lax.all_to_all(send, "mp", 0, 0, tiled=True)
    coords, keep, give = pl.pallas_call(
        gram_kernel,
        out_shape=(
            jax.ShapeDtypeStruct((160, 128), BF16),
            jax.ShapeDtypeStruct((HALF, 128), BF16),
            jax.ShapeDtypeStruct((HALF, 128), BF16),
        ),
        in_specs=[vmem],
        out_specs=(vmem, vmem, vmem),
        scratch_shapes=[pltpu.VMEM((FB, 256), BF16), pltpu.VMEM((2 * HALF, 128), BF16)],
        compiler_params=pltpu.CompilerParams(vmem_limit_bytes=12 << 20),
        name="gram",
    )(recv)
    features = pl.pallas_call(
        features_kernel,
        out_shape=jax.ShapeDtypeStruct((32, 4096), BF16),
        in_specs=[vmem, vmem],
        out_specs=vmem,
        cost_estimate=pl.CostEstimate(flops=2 * 32 * 64 * 4096, bytes_accessed=300000, transcendentals=0),
        compiler_params=pltpu.CompilerParams(vmem_limit_bytes=12 << 20),
        name="features",
    )(assign, coords)
    total = keep + lax.ppermute(give, "dp", moves(lambda y, x, c: (y, x, 1 - c)))
    for ring in (lambda y, x, c, k: (y, (x + k) % 4, c), lambda y, x, c, k: ((y + k) % 4, x, c)):
        after, before, across = (
            lax.ppermute(total, "dp", moves(functools.partial(ring, k=k))).astype(F32) for k in (1, 3, 2))
        total = ((total.astype(F32) + across) + (after + before)).astype(BF16)
        total, features = lax.optimization_barrier((total, features))
    other = lax.ppermute(total, "dp", moves(lambda y, x, c: (y, x, 1 - c)))
    factor = pl.pallas_call(
        factor_kernel,
        out_shape=jax.ShapeDtypeStruct((FB, FB), F32),
        in_specs=[vmem, vmem],
        out_specs=hbm,
        scratch_shapes=[
            pltpu.VMEM((FB, FB), F32),
            pltpu.VMEM((2 * HALF, 128), BF16),
            pltpu.VMEM((1280, 128), F32),
            pltpu.VMEM((128, 128), F32),
            pltpu.SemaphoreType.DMA((4,)),
        ],
        compiler_params=pltpu.CompilerParams(vmem_limit_bytes=12 << 20),
        name="factor",
    )(total, other).reshape(1, FB, FB)
    return features, factor


def solution(mesh):
    return jax.shard_map(
        shards,
        mesh=mesh,
        in_specs=(P("dp", "mp"), P("dp", "mp"), P(), P(), P(), P("dp", None)),
        out_specs=(P(("dp", "mp"), None), P("mp", None, None)),
        check_vma=False,
    )
```
